128 devices in a mesh: dp: 32 (over z, x, core), head: 4 (over y).
Axes of the slice: x: 4, y: 4, z: 4, core: 2. Of those that a mesh axis runs over, the one named last changes fastest.
Arguments:
- hidden: bfloat16 [1024, 2048], P('dp'), may hold values from -6 to 6
- attn_gain: float32 [2048], replicated, may hold values from 0.1 to 1.9
- w_query: bfloat16 [2048, 3072], P(None, 'head'), may hold values from -0.125 to 0.125
- w_latent: bfloat16 [2048, 576], P(None, 'head'), may hold values from -0.125 to 0.125
- latent_gain: float32 [512], replicated, may hold values from 0.1 to 1.9
- w_key_up: bfloat16 [16, 128, 512], P('head'), may hold values from -0.5 to 0.5
- w_value_up: bfloat16 [16, 512, 128], P('head'), may hold values from -0.25 to 0.25
- w_out: bfloat16 [2048, 2048], P('head'), may hold values from -0.125 to 0.125
- kv_cache: bfloat16 [1024, 128, 576], P('dp'), may hold values from -110 to 110
- lengths: int32 [1024], P('dp'), may hold values from 1 to 128, 65536 in all
- live_mask: int32 [1024], P('dp'), may hold values 0 or 1
- mlp_gain: float32 [2048], replicated, may hold values from 0.1 to 1.9
- w_router: bfloat16 [2048, 64], replicated, may hold values from -0.125 to 0.125
- routes: int32 [1024, 6], P('dp'), may hold values from 0 to 63, all different within a row; in each aligned block of 32 rows (0 to 31, 32 to 63, ...) at most 6 rows name the same one
- w_experts_in: bfloat16 [64, 2048, 2, 1408], P('dp', None, None, 'head'), may hold values from -0.125 to 0.125
- w_experts_out: bfloat16 [64, 1408, 2048], P('dp', 'head'), may hold values from -0.15625 to 0.15625
- w_shared_in: bfloat16 [2048, 2, 1408], P(None, None, 'head'), may hold values from -0.125 to 0.125
- w_shared_out: bfloat16 [1408, 2048], P('head'), may hold values from -0.15625 to 0.15625
Outputs:
- output: bfloat16 [1024, 2048], P('dp', 'head')
The draws below stay inside these ranges and needn't reach their ends.
Inputs may be any that keep to these rules, and one draw needn't show every extreme that they name: Among the routes of one device's 32 rows no expert is named more than 6 times, a bound that some block reaches. Request t has cached positions 0 to lengths[t] - 1; some request has 128.
All inputs are finite; a program needn't handle non-finite values. No bound on the sum of `lengths` or of `live_mask` on one device may be relied on, other than what follows from the above.
Results may differ from the reference program's by a relative error of at most 0.02.
The reference program's roundings to bfloat16 on the way count: a program that leaves them out, or rounds other values in their place, can miss the bound.
Values may be sent and summed in bfloat16 or wider, within the bound.
A program may use at most 128 MiB of HBM per device.

```python
import math
import jax
import jax.numpy as jnp
import numpy as np
from jax import lax

D = 2048
H = 16
NOPE = 128
ROPE = 64
VDIM = 128
LAT = 512
FF = 1408
SFF = 1408
TOPK = 6
REQ_DEV = 32
CTX = 128
EXPERTS = 64
TOKENS = 1024
CAP = 6
N_DP = 32
N_HEAD = 4


def draw_kv_cache(key, part):
    full_shape = (TOKENS, CTX, LAT + ROPE)
    keys_all = jax.random.split(key, 5)
    result = jnp.clip(jax.random.normal(keys_all[4], full_shape, jnp.float32), -4.0, 4.0)
    return result.astype(jnp.bfloat16)


def place_ends(array, key, low, high):
    place = [jax.random.randint(jax.random.fold_in(key, axis), (), 0, length) for axis, length in enumerate(array.shape)]
    main_axis = array.shape.index(max(array.shape))
    beside = place[:main_axis] + [(place[main_axis] + 1) % array.shape[main_axis]] + place[main_axis + 1:]
    return array.at[tuple(place)].set(low).at[tuple(beside)].set(high)


def levels(stream_key, extent, pieces, low, top_value):
    def one(axis_at, parts):
        heights = jax.random.uniform(jax.random.fold_in(jax.random.fold_in(stream_key, 6), axis_at), (parts,), jnp.float32, low / len(pieces), top_value / len(pieces))
        return jnp.repeat(jnp.exp(heights), extent[axis_at] // parts).reshape((-1,) + (1,) * (len(extent) - axis_at - 1))

    loudness = one(*pieces[0])
    for cut in pieces[1:]:
        loudness = loudness * one(*cut)
    return loudness


def profile(number_of, total, reach, lean):
    loads = [(1 << 20) // math.isqrt(standing ** lean) + 1 for standing in range(2, number_of + 1)]
    rest, counts = total - reach - (number_of - 1), [1] * (number_of - 1)
    while rest > 0:
        candidates = [i for i in range(number_of - 1) if counts[i] < reach]
        pool, left = sum([loads[i] for i in candidates]), rest
        for i in candidates:
            extra = min(reach - counts[i], max(1, left * loads[i] // pool), rest)
            counts[i] = counts[i] + extra
            rest = rest - extra
    return np.array([reach] + counts)


def ragged(stream_key, number_of, total, bound, lean):
    if number_of == 2:
        one = jax.random.randint(stream_key, (), max(1, total - bound), min(bound, total - 1) + 1)
        return jnp.stack([one, total - one])
    sizes = jnp.asarray(profile(number_of, total, bound, lean), jnp.int32)
    couples = (number_of - 1) // 2
    source_of, taker = sizes[1:1 + 2 * couples:2], sizes[2:2 + 2 * couples:2]
    margin = jnp.minimum(source_of - 1, bound - taker)
    shifted = jax.random.randint(jax.random.fold_in(stream_key, 1), (couples,), 0, 1 << 20) % (margin + 1)
    sizes = sizes.at[1:1 + 2 * couples:2].set(source_of - shifted).at[2:2 + 2 * couples:2].set(taker + shifted)
    return sizes[jax.random.permutation(jax.random.fold_in(stream_key, 2), number_of)]


def routed_block(key, own, number, rows, count, top, reach, lean):
    order = jax.random.permutation(key, count)
    crowded, usual = shares(count, rows * top, reach, lean, True), shares(count, rows * top, reach, lean, False)
    places = jnp.arange(count)

    def named(tallies, rotation):
        used = int((tallies > 0).sum())
        fixed = max(1, used // 4)
        shifted = fixed + (places - fixed + rotation * (used - fixed)) % max(1, count - fixed)
        return jnp.zeros((count,), jnp.int32).at[order[jnp.where(places < fixed, places, shifted)]].set(jnp.asarray(tallies, jnp.int32))

    tallies = jnp.where(number % 4 == 0, named(crowded, number // 4), named(usual, number - number // 4 - 1))
    mixed = jax.random.permutation(jax.random.fold_in(own, 3), count)
    source_of, sink = mixed[0:count // 2 * 2:2], mixed[1:count // 2 * 2:2]
    margin = jnp.minimum(tallies[source_of] - 1, reach - tallies[sink]) // 2
    margin = jnp.where((source_of == order[0]) | (sink == order[0]) | (tallies[sink] == 0), 0, jnp.maximum(margin, 0))
    shifted = jax.random.randint(jax.random.fold_in(own, 4), (count // 2,), 0, 1 << 20) % (margin + 1)
    tallies = tallies.at[source_of].add(-shifted).at[sink].add(shifted)
    items = jnp.searchsorted(jnp.cumsum(tallies), jnp.arange(rows * top), side="right").astype(jnp.int32)
    table = items.reshape(top, rows).T
    table = table[jax.random.permutation(jax.random.fold_in(own, 1), rows)]
    rotation = jax.random.randint(jax.random.fold_in(own, 2), (rows, 1), 0, top)
    return jnp.take_along_axis(table, (jnp.arange(top)[None, :] + rotation) % top, axis=1)


def shares(count, total, most, slope, full):
    loads = [(1 << 20) // math.isqrt(rank ** slope) + 1 for rank in range(1, count + 1)]
    largest = most if full else min(most, max(-(-total // count), total * loads[0] // sum(loads)))
    least = 1 if total - largest >= count - 1 else 0
    holding, rest = [largest] + [least] * (count - 1), total - largest - least * (count - 1)
    while rest > 0:
        free = [i for i in range(1, count) if holding[i] < largest] or [i for i in range(1, count) if holding[i] < most]
        pool, left = sum([loads[i] for i in free]), rest
        for i in free:
            extra = min(most - holding[i], max(1, left * loads[i] // pool), rest)
            holding[i] = holding[i] + extra
            rest = rest - extra
    return np.array(holding)


def bell_draw(key, shape, scale, bound, shards=(), kind=jnp.bfloat16):
    entries = scale * jax.random.normal(key, shape, jnp.float32)
    if shards:
        entries = entries * levels(key, shape, shards, -0.22, 0.18)
    return jnp.clip(entries, -bound, bound).astype(kind)


def setup_inputs(seed: int = 0) -> dict:
    splits = jax.random.split(jax.random.key(seed), 19)
    hidden = bell_draw(splits[0], (TOKENS, D), 1.0, 6.0, ((0, 32),))
    attn_gain = jnp.clip(1.0 + 0.18 * jax.random.normal(splits[1], (D,), jnp.float32), 0.1, 1.9)
    w_query = bell_draw(splits[2], (D, H * (NOPE + ROPE)), D ** -0.5, 0.125, ((1, 4),))
    w_latent = bell_draw(splits[3], (D, LAT + ROPE), D ** -0.5, 0.125, ((1, 4),))
    latent_gain = jnp.clip(1.0 + 0.18 * jax.random.normal(splits[4], (LAT,), jnp.float32), 0.1, 1.9)
    w_key_up = bell_draw(splits[5], (H, NOPE, LAT), NOPE ** -0.5, 0.5, ((0, 4),))
    w_value_up = bell_draw(splits[6], (H, LAT, VDIM), LAT ** -0.5, 0.25, ((0, 4),))
    w_out = bell_draw(splits[7], (H * VDIM, D), (H * VDIM) ** -0.5, 0.125, ((0, 4),))
    kv_cache = draw_kv_cache(jax.random.fold_in(splits[18], 71), 0)
    lengths = ragged(splits[9], TOKENS, TOKENS * CTX // 2, CTX, 2).astype(jnp.int32)
    live_mask = place_ends((jax.random.randint(splits[10], (TOKENS,), 0, 8) < 7).astype(jnp.int32), jax.random.fold_in(splits[10], 1), 0, 1)
    mlp_gain = jnp.clip(1.0 + 0.18 * jax.random.normal(splits[11], (D,), jnp.float32), 0.1, 1.9)
    w_router = bell_draw(splits[12], (D, EXPERTS), D ** -0.5, 0.125)
    routes_keys = jax.random.split(jax.random.fold_in(splits[13], 1), TOKENS // REQ_DEV)
    routes_turns = jax.random.permutation(jax.random.fold_in(splits[13], 3), TOKENS // REQ_DEV)
    routes = jax.vmap(lambda own, number: routed_block(jax.random.fold_in(splits[13], 2), own, number, REQ_DEV, EXPERTS, TOPK, CAP, 2))(routes_keys, routes_turns).reshape((TOKENS, TOPK))
    w_experts_in = bell_draw(splits[14], (EXPERTS, D, 2, FF), D ** -0.5, 0.125, ((0, 32), (3, 4)))
    w_experts_out = bell_draw(splits[15], (EXPERTS, FF, D), FF ** -0.5, 0.15625, ((0, 32), (1, 4)))
    w_shared_in = bell_draw(splits[16], (D, 2, SFF), D ** -0.5, 0.125, ((2, 4),))
    w_shared_out = bell_draw(splits[17], (SFF, D), SFF ** -0.5, 0.15625, ((0, 4),))
    return dict(hidden=hidden, attn_gain=attn_gain, w_query=w_query, w_latent=w_latent, latent_gain=latent_gain, w_key_up=w_key_up, w_value_up=w_value_up, w_out=w_out, kv_cache=kv_cache, lengths=lengths, live_mask=live_mask, mlp_gain=mlp_gain, w_router=w_router, routes=routes, w_experts_in=w_experts_in, w_experts_out=w_experts_out, w_shared_in=w_shared_in, w_shared_out=w_shared_out)


norm_eps = 1e-06
rope_theta = 50000.0
route_scale = 2.446

def rms_norm(values, weights):
    mean_square = lax.optimization_barrier(jnp.mean(values * values, axis=-1, keepdims=True))
    return values * lax.rsqrt(mean_square + norm_eps) * weights

def rotary(values, positions):
    half_size = values.shape[-1] // 2
    frequency = rope_theta ** (-jnp.arange(half_size, dtype=jnp.float32) / half_size)
    angles = positions.reshape((-1,) + (1,) * (values.ndim - 1)) * frequency
    first_half = values[..., :half_size]
    second_half = values[..., half_size:]
    cosine = jnp.cos(angles)
    sine_part = jnp.sin(angles)
    return jnp.concatenate([first_half * cosine - second_half * sine_part, second_half * cosine + first_half * sine_part], axis=-1)

def reference(hidden, attn_gain, w_query, w_latent, latent_gain, w_key_up, w_value_up, w_out, kv_cache, lengths, live_mask, mlp_gain, w_router, routes, w_experts_in, w_experts_out, w_shared_in, w_shared_out):
    token_count = hidden.shape[0]
    normed = rms_norm(hidden.astype(jnp.float32), attn_gain).astype(jnp.bfloat16)
    query_all = jnp.dot(normed, w_query, preferred_element_type=jnp.float32).reshape(token_count, H, NOPE + ROPE)
    positions = lengths.astype(jnp.float32)
    query_nope = query_all[..., :NOPE].astype(jnp.bfloat16)
    query_rope = rotary(query_all[..., NOPE:], positions).astype(jnp.bfloat16)
    query_latent = jnp.einsum('thn,hnc->thc', query_nope.astype(jnp.float32), w_key_up.astype(jnp.float32)).astype(jnp.bfloat16)
    fresh_kv = jnp.dot(normed, w_latent, preferred_element_type=jnp.float32).astype(jnp.bfloat16)
    latent_new = rms_norm(fresh_kv[:, :LAT].astype(jnp.float32), latent_gain)
    rope_new = rotary(fresh_kv[:, LAT:].astype(jnp.float32), positions)
    key_new = jnp.concatenate([latent_new, rope_new], axis=-1).astype(jnp.bfloat16)
    query_full = jnp.concatenate([query_latent, query_rope], axis=-1).astype(jnp.float32)
    inverse_root = 1.0 / math.sqrt(NOPE + ROPE)
    cache_wide = kv_cache.astype(jnp.float32)
    scores = jnp.einsum('thc,tjc->thj', query_full, cache_wide) * inverse_root
    in_cache = jnp.arange(CTX, dtype=jnp.int32)[None, :] < lengths[:, None]
    scores = jnp.where(in_cache[:, None, :], scores, -jnp.inf)
    score_new = jnp.einsum('thc,tc->th', query_full, key_new.astype(jnp.float32)) * inverse_root
    highest = jnp.maximum(lax.optimization_barrier(jnp.max(scores, axis=-1)), score_new)
    weights_cached = jnp.exp(scores - highest[..., None])
    weight_new = jnp.exp(score_new - highest)
    denominator = lax.optimization_barrier(jnp.sum(weights_cached, axis=-1)) + weight_new
    probabilities = (weights_cached / denominator[..., None]).astype(jnp.bfloat16)
    prob_new = (weight_new / denominator).astype(jnp.bfloat16)
    context = jnp.einsum('thj,tjc->thc', probabilities.astype(jnp.float32), cache_wide[..., :LAT])
    context = context + prob_new.astype(jnp.float32)[..., None] * key_new[:, None, :LAT].astype(jnp.float32)
    context = context.astype(jnp.bfloat16)
    values = jnp.einsum('thc,hcv->thv', context.astype(jnp.float32), w_value_up.astype(jnp.float32)).astype(jnp.bfloat16)
    attention = jnp.dot(values.reshape(token_count, H * VDIM), w_out, preferred_element_type=jnp.float32)
    mixed_rows = (hidden.astype(jnp.float32) + attention).astype(jnp.bfloat16)
    ffn_input = rms_norm(mixed_rows.astype(jnp.float32), mlp_gain).astype(jnp.bfloat16)
    logits = jnp.dot(ffn_input, w_router, preferred_element_type=jnp.float32)
    chosen = jax.nn.sigmoid(jnp.take_along_axis(logits, routes, axis=1))
    route_weight = route_scale * live_mask.astype(jnp.float32)[:, None] * chosen / lax.optimization_barrier(jnp.sum(chosen, axis=1, keepdims=True))
    shared_pair = jnp.dot(ffn_input, w_shared_in.reshape(D, 2 * SFF), preferred_element_type=jnp.float32).reshape(token_count, 2, SFF)
    shared_act = (jax.nn.silu(shared_pair[:, 0]) * shared_pair[:, 1]).astype(jnp.bfloat16)
    shared_out = jnp.dot(shared_act, w_shared_out, preferred_element_type=jnp.float32)
    pair_count = token_count * TOPK
    flat_routes = routes.reshape(pair_count)
    slot_total = N_DP * CAP

    def one_expert(collected, expert):
        chosen_pairs = jnp.nonzero(flat_routes == expert, size=slot_total, fill_value=pair_count)[0].astype(jnp.int32)
        token_rows = ffn_input[jnp.minimum(chosen_pairs, pair_count - 1) // TOPK]
        gate_up = jnp.dot(token_rows, w_experts_in[expert].reshape(D, 2 * FF), preferred_element_type=jnp.float32).reshape(slot_total, 2, FF)
        acting = (jax.nn.silu(gate_up[:, 0]) * gate_up[:, 1]).astype(jnp.bfloat16)
        blocks = jnp.einsum('snf,nfd->snd', acting.reshape(slot_total, N_HEAD, FF // N_HEAD).astype(jnp.float32), w_experts_out[expert].reshape(N_HEAD, FF // N_HEAD, D).astype(jnp.float32))
        blocks = lax.optimization_barrier(blocks.astype(jnp.bfloat16)).astype(jnp.float32)
        expert_rows = lax.optimization_barrier(jnp.sum(blocks, axis=1)).astype(jnp.bfloat16)
        collected = collected.at[chosen_pairs].set(expert_rows, mode='drop')
        return (collected, None)
    expert_out, unused = lax.scan(one_expert, jnp.zeros((pair_count, D), jnp.bfloat16), jnp.arange(EXPERTS, dtype=jnp.int32))
    routed = lax.optimization_barrier(jnp.sum(route_weight[..., None] * expert_out.reshape(token_count, TOPK, D).astype(jnp.float32), axis=1))
    return (mixed_rows.astype(jnp.float32) + shared_out + routed).astype(jnp.bfloat16)
```

```python
import functools
import math

import jax
import jax.numpy as jnp
from jax import lax
from jax.experimental import pallas as pl
from jax.experimental.pallas import tpu as pltpu
from jax.sharding import PartitionSpec as P

NOPE = 128
ROPE = 64
VDIM = 128
LAT = 512

norm_eps = 1e-06
rope_theta = 50000.0
route_scale = 2.446

MESH = pl.DeviceIdType.MESH
BF = jnp.bfloat16
F32 = jnp.float32
NT = (((1,), (1,)), ((), ()))
TN = (((0,), (0,)), ((), ()))


def rms_norm(values, weights):
    mean_square = jnp.mean(values * values, axis=-1, keepdims=True)
    return values * lax.rsqrt(mean_square + norm_eps) * weights


def rotary(values, positions):
    half_size = values.shape[-1] // 2
    frequency = rope_theta ** (-jnp.arange(half_size, dtype=jnp.float32) / half_size)
    angles = positions.reshape((-1,) + (1,) * (values.ndim - 1)) * frequency
    first_half = values[..., :half_size]
    second_half = values[..., half_size:]
    cosine = jnp.cos(angles)
    sine_part = jnp.sin(angles)
    return jnp.concatenate(
        [
            first_half * cosine - second_half * sine_part,
            second_half * cosine + first_half * sine_part,
        ],
        axis=-1,
    )


def head_gather_kernel(x_ref, o_ref, ssem, rsem):
    dp, h = lax.axis_index("dp"), lax.axis_index("head")
    barrier = pltpu.get_barrier_semaphore()
    for k in range(1, 4):
        pl.semaphore_signal(barrier, inc=1, device_id=(dp, lax.rem(h + k, 4)), device_id_type=MESH)
    pl.semaphore_wait(barrier, 3)
    copies = []
    for k in range(1, 4):
        copies.append(
            pltpu.make_async_remote_copy(
                src_ref=x_ref,
                dst_ref=o_ref.at[h],
                send_sem=ssem.at[k - 1],
                recv_sem=rsem.at[k - 1],
                device_id=(dp, lax.rem(h + k, 4)),
                device_id_type=MESH,
            )
        )
        copies[-1].start()
    o_ref[h] = x_ref[...]
    for k in range(1, 4):
        pltpu.make_async_remote_copy(
            src_ref=x_ref,
            dst_ref=o_ref.at[lax.rem(h + 4 - k, 4)],
            send_sem=ssem.at[k - 1],
            recv_sem=rsem.at[k - 1],
            device_id=(dp, lax.rem(h + k, 4)),
            device_id_type=MESH,
        ).wait()


def head_gather(x):
    return pl.pallas_call(
        head_gather_kernel,
        out_shape=jax.ShapeDtypeStruct((4,) + x.shape, x.dtype),
        in_specs=[pl.BlockSpec(memory_space=pltpu.VMEM)],
        out_specs=pl.BlockSpec(memory_space=pltpu.VMEM),
        scratch_shapes=[pltpu.SemaphoreType.DMA((3,)), pltpu.SemaphoreType.DMA((3,))],
        compiler_params=pltpu.CompilerParams(collective_id=0, has_side_effects=True),
    )(x)


def moe_kernel(
    part_ref, hid_ref, gain_ref, rt_ref, routes_ref, live_ref, win_hbm, wout_hbm, sin_hbm, sout_hbm,
    out_ref,
    win, wout, sin, sout, yrs, mix, ffn, xb, shared, xs, hid_slot, outs, pmat, wslot, cb, pr, rl, rf, al, af, fin, tot, yr,
    wsem, ssem, rsem,
):
    dp, h = lax.axis_index("dp"), lax.axis_index("head")
    core = lax.rem(dp, 2)
    x = lax.rem(dp // 2, 4)
    z = dp // 8
    a = x + core * (z - x)
    b = z + core * (x - z)
    sa, sb = 2 + 6 * core, 8 - 6 * core
    na, nb = 1 + 3 * core, 4 - 3 * core

    def dev(da, db):
        return (lax.rem(a + da + 4, 4) * sa + lax.rem(b + db + 4, 4) * sb + core, h)

    def num(da, db):
        return lax.rem(a + da + 4, 4) * na + lax.rem(b + db + 4, 4) * nb

    partner = (dp + 1 - 2 * core, h)

    def ypeer(k):
        return (dp, lax.rem(h + k, 4))

    weights = [
        pltpu.make_async_copy(s, d, wsem.at[i])
        for i, (s, d) in enumerate(((sin_hbm, sin), (sout_hbm, sout), (win_hbm, win), (wout_hbm, wout)))
    ]
    for copy in weights:
        copy.start()

    barrier = pltpu.get_barrier_semaphore()
    for peer in (ypeer(1), ypeer(2), ypeer(3), dev(1, 0), dev(-1, 0), dev(0, 1), dev(0, -1), partner):
        pl.semaphore_signal(barrier, inc=1, device_id=peer, device_id_type=MESH)
    pl.semaphore_wait(barrier, 8)

    pending = []

    def send(i, src, dst, peer):
        copy = pltpu.make_async_remote_copy(
            src_ref=src, dst_ref=dst, send_sem=ssem.at[i], recv_sem=rsem.at[i], device_id=peer, device_id_type=MESH
        )
        copy.start()
        pending.append(copy)

    def recv(i, dst):
        pltpu.make_async_remote_copy(
            src_ref=dst, dst_ref=dst, send_sem=ssem.at[i], recv_sem=rsem.at[i], device_id=partner, device_id_type=MESH
        ).wait_recv()

    for k in range(1, 4):
        column = pl.multiple_of(lax.rem(h + k, 4) * 512, 512)
        send(k - 1, part_ref.at[:, pl.ds(column, 512)], yrs.at[k - 1], ypeer(k))
    own = pl.ds(pl.multiple_of(h * 512, 512), 512)
    attention = part_ref[:, own].astype(F32)
    for k in range(1, 4):
        recv(k - 1, yrs.at[k - 1])
        attention = attention + yrs[k - 1].astype(F32)
    mix[h] = (hid_ref[:, own].astype(F32) + attention).astype(BF)
    for k in range(1, 4):
        send(2 + k, mix.at[h], mix.at[h], ypeer(k))
    for k in range(1, 4):
        recv(2 + k, mix.at[lax.rem(h + 4 - k, 4)])
    square = jnp.zeros((32, 1), F32)
    for i in range(4):
        v = mix[i].astype(F32)
        square = square + jnp.sum(v * v, axis=1, keepdims=True)
    scale = lax.rsqrt(square * (1.0 / 2048.0) + norm_eps)
    for i in range(4):
        v = mix[i].astype(F32)
        ffn[:, i * 512 : (i + 1) * 512] = (v * scale * gain_ref[:, i * 512 : (i + 1) * 512]).astype(BF)

    logits = lax.dot_general(rt_ref[...], ffn[...], NT, preferred_element_type=F32)
    expert_id = lax.broadcasted_iota(jnp.int32, (64, 32), 0)
    named = expert_id == routes_ref[0:1, :]
    for k in range(1, 6):
        named = named | (expert_id == routes_ref[k : k + 1, :])
    chosen = jnp.where(named, jax.nn.sigmoid(logits), 0.0)
    weight = route_scale * live_ref[...].astype(F32) * chosen / jnp.sum(chosen, axis=0, keepdims=True)
    w_hi = weight.astype(BF)
    w_lo = (weight - w_hi.astype(F32)).astype(BF)
    eye = (lax.broadcasted_iota(jnp.int32, (32, 32), 0) == lax.broadcasted_iota(jnp.int32, (32, 32), 1)).astype(F32).astype(BF)
    extra = lax.dot_general(eye, jnp.concatenate([w_hi, w_lo], axis=0), NT, preferred_element_type=F32).astype(BF)

    me = num(0, 0)
    rows = pl.ds(pl.multiple_of(me * 64 + core * 32, 32), 32)
    for half in range(2):
        xb[half, rows, 0:1024] = ffn[:, half * 1024 : (half + 1) * 1024]
        xb[half, rows, 1024:1152] = extra

    def block(n, low=0, count=64):
        return xb.at[core, pl.ds(pl.multiple_of(n * 64 + low, 32), count), :]

    def other(n):
        return xb.at[1 - core, pl.ds(pl.multiple_of(n * 64, 32), 64), :]

    G = 8
    PT = G + 20
    send(PT, xb.at[1 - core, rows, :], xb.at[1 - core, rows, :], partner)
    send(PT + 1, xb.at[core, rows, :], xb.at[core, rows, :], partner)
    prow = pl.ds(pl.multiple_of(me * 64 + (1 - core) * 32, 32), 32)
    recv(PT, xb.at[core, prow, :])

    order = (0, -1, 1, 2)

    def spread(j):
        base = G + 4 + 4 * j
        send(base, block(num(order[j], 0)), block(num(order[j], 0)), dev(0, 1))
        send(base + 1, block(num(order[j], 0)), block(num(order[j], 0)), dev(0, -1))

    def to_partner(j, o):
        if (j, o) != (0, 0):
            n = num(order[j], order[o])
            send(PT + 1 + 4 * j + o, block(n), block(n), partner)

    send(G, block(me), block(me), dev(1, 0))
    send(G + 1, block(me), block(me), dev(-1, 0))
    spread(0)

    weights[0].wait()
    weights[1].wait()
    gate = lax.dot_general(ffn[...], sin[0], NT, preferred_element_type=F32)
    up = lax.dot_general(ffn[...], sin[1], NT, preferred_element_type=F32)
    act = (gate / (1.0 + jnp.exp(-gate)) * up).astype(BF)
    for i in range(4):
        shared[i] = jnp.dot(act, sout[:, i * 512 : (i + 1) * 512], preferred_element_type=F32)

    recv(G, block(num(-1, 0)))
    n = num(-1, 0)
    send(G + 2, block(n, 0, 32), block(n, 0, 32), dev(1, 0))
    spread(1)
    recv(G + 1, block(num(1, 0)))
    n = num(1, 0)
    send(G + 3, block(n, 32, 32), block(n, 32, 32), dev(-1, 0))
    spread(2)

    def first(j):
        base = G + 4 + 4 * j
        n = num(order[j], -1)
        recv(base, block(n))
        send(base + 2, block(n, 0, 32), block(n, 0, 32), dev(0, 1))
        n = num(order[j], 1)
        recv(base + 1, block(n))
        send(base + 3, block(n, 32, 32), block(n, 32, 32), dev(0, -1))
        to_partner(j, 1)
        to_partner(j, 2)

    def second(j):
        base = G + 4 + 4 * j
        n = num(order[j], 2)
        recv(base + 2, block(n, 0, 32))
        recv(base + 3, block(n, 32, 32))
        to_partner(j, 3)

    first(0)
    recv(G + 2, block(num(2, 0), 0, 32))
    recv(G + 3, block(num(2, 0), 32, 32))
    spread(3)
    for j in range(1, 4):
        to_partner(j, 0)
    second(0)
    first(1)
    first(2)
    second(1)
    first(3)
    second(2)
    second(3)

    prow2 = pl.ds(pl.multiple_of(me * 64 + (1 - core) * 32, 32), 32)
    recv(PT + 1, xb.at[1 - core, prow2, :])
    for j in range(4):
        for o in range(4):
            if (j, o) != (0, 0):
                recv(PT + 1 + 4 * j + o, other(num(order[o], order[j])))

    lane = lax.broadcasted_iota(jnp.int32, (8, 128), 1)
    row = lax.broadcasted_iota(jnp.int32, (8, 128), 0)
    target = 2 * dp + lax.rem(row, 2) + 64 * (row // 2)
    pick = jnp.where((lane == target) & (row < 4), 1.0, 0.0).astype(BF)
    t_from = lax.broadcasted_iota(jnp.int32, (256, 256), 0)
    t_to = lax.broadcasted_iota(jnp.int32, (256, 256), 1)
    before = jnp.where((t_from < t_to) & (t_from // 32 == t_to // 32), 1.0, 0.0).astype(BF)
    source = lax.broadcasted_iota(jnp.int32, (1, 256), 1) // 32
    slot = lax.broadcasted_iota(jnp.int32, (64, 256), 0)
    for g in range(4):
        info = lax.dot_general(pick, xb[0, g * 256 : (g + 1) * 256, 1024:1152], NT, preferred_element_type=F32)
        mask = jnp.where(info != 0.0, 1.0, 0.0)
        rank = jnp.dot(mask.astype(BF), before, preferred_element_type=F32)
        for e in range(2):
            value = info[e : e + 1, :] + info[2 + e : 3 + e, :]
            place = jnp.where(mask[e : e + 1, :] > 0.0, 8 * source + rank[e : e + 1, :].astype(jnp.int32), -1)
            hit = jnp.where(slot == place, 1.0, 0.0)
            wslot[e, g * 64 : (g + 1) * 64, :] = jnp.broadcast_to(
                jnp.sum(hit * value, axis=1, keepdims=True), (64, 128)
            )
            hit = hit.astype(BF)
            pmat[g, e * 64 : (e + 1) * 64, :] = hit
        for half in range(2):
            got = jnp.dot(
                pmat[g], xb[half, g * 256 : (g + 1) * 256, 0:1024], preferred_element_type=F32
            ).astype(BF)
            for e in range(2):
                xs[e, g * 64 : (g + 1) * 64, half * 1024 : (half + 1) * 1024] = got[e * 64 : (e + 1) * 64]

    weights[2].wait()
    weights[3].wait()
    for e in range(2):
        gate = lax.dot_general(xs[e], win[2 * e], NT, preferred_element_type=F32)
        up = lax.dot_general(xs[e], win[2 * e + 1], NT, preferred_element_type=F32)
        hid_slot[...] = (gate / (1.0 + jnp.exp(-gate)) * up).astype(BF)
        for i in range(4):
            result = jnp.dot(hid_slot[...], wout[e, :, i * 512 : (i + 1) * 512], preferred_element_type=F32)
            result = (result * wslot[e, :, 0:1]).astype(BF)
            for g in range(4):
                outs[g, e * 64 : (e + 1) * 64, i * 512 : (i + 1) * 512] = result[g * 64 : (g + 1) * 64]

    R = PT + 17
    for g in range(4):
        for half in range(2):
            cb[half, g * 256 : (g + 1) * 256, :] = lax.dot_general(
                pmat[g], outs[g, :, half * 1024 : (half + 1) * 1024], TN, preferred_element_type=F32
            ).astype(BF)
        span = pl.ds(g * 256, 256)
        send(R + g, cb.at[1 - core, span, :], pr.at[span, :], partner)
    for g in range(4):
        span = pl.ds(g * 256, 256)
        recv(R + g, pr.at[span, :])
        cb[core, span, :] = (cb[core, span, :].astype(F32) + pr[span, :].astype(F32)).astype(BF)

    def cpart(n, low=0, count=64):
        return pl.ds(pl.multiple_of(n * 64 + low, 32), count)

    def ring(base, here, ahead, behind, far, up_dev, down_dev, lows, fulls, stage):
        if stage == 0:
            send(base, cb.at[core, cpart(far, 0, 32), :], lows.at[0], up_dev)
            send(base + 1, cb.at[core, cpart(far, 32, 32), :], lows.at[1], down_dev)
        elif stage == 1:
            recv(base, lows.at[0])
            s = cpart(ahead, 0, 32)
            cb[core, s, :] = (cb[core, s, :].astype(F32) + lows[0].astype(F32)).astype(BF)
            send(base + 2, cb.at[core, cpart(ahead), :], fulls.at[0], up_dev)
            recv(base + 1, lows.at[1])
            s = cpart(behind, 32, 32)
            cb[core, s, :] = (cb[core, s, :].astype(F32) + lows[1].astype(F32)).astype(BF)
            send(base + 3, cb.at[core, cpart(behind), :], fulls.at[1], down_dev)
        else:
            recv(base + 2, fulls.at[0])
            recv(base + 3, fulls.at[1])
            s = cpart(here)
            cb[core, s, :] = (cb[core, s, :].astype(F32) + fulls[0].astype(F32) + fulls[1].astype(F32)).astype(BF)

    S = R + 4
    back = (2, 1, -1, 0)

    def bring(j, stage):
        d = back[j]
        ring(S + 4 * j, num(d, 0), num(d, 1), num(d, -1), num(d, 2), dev(0, 1), dev(0, -1), rl.at[j], rf.at[j], stage)

    def aring(stage):
        ring(S + 16, num(0, 0), num(1, 0), num(-1, 0), num(2, 0), dev(1, 0), dev(-1, 0), al, af, stage)

    for j in range(4):
        bring(j, 0)
    for j in range(4):
        bring(j, 1)
    bring(0, 2)
    aring(0)
    bring(1, 2)
    bring(2, 2)
    aring(1)
    bring(3, 2)
    aring(2)

    F = S + 20
    send(F, cb.at[core, prow, :], fin, partner)
    for i in range(2):
        tot[2 * core + i] = (shared[2 * core + i] + cb[core, rows, i * 512 : (i + 1) * 512].astype(F32)).astype(BF)
    recv(F, fin)
    for i in range(2):
        tot[2 * (1 - core) + i] = (shared[2 * (1 - core) + i] + fin[:, i * 512 : (i + 1) * 512].astype(F32)).astype(BF)
    for k in range(1, 4):
        send(F + k, tot.at[lax.rem(h + k, 4)], yr.at[k - 1], ypeer(k))
    result = mix[h].astype(F32) + tot[h].astype(F32)
    for k in range(1, 4):
        recv(F + k, yr.at[k - 1])
        result = result + yr[k - 1].astype(F32)
    out_ref[...] = result.astype(BF)
    for copy in pending:
        copy.wait_send()


MESSAGES = 8 + 20 + 17 + 4 + 20 + 4


def moe(part, hidden, gain, router_t, routes_t, live, win, wout, sin, sout):
    vmem = pl.BlockSpec(memory_space=pltpu.VMEM)
    hbm = pl.BlockSpec(memory_space=pl.ANY)
    return pl.pallas_call(
        moe_kernel,
        out_shape=jax.ShapeDtypeStruct((32, 512), BF),
        in_specs=[vmem] * 6 + [hbm] * 4,
        out_specs=vmem,
        scratch_shapes=[
            pltpu.VMEM((4, 352, 2048), BF),
            pltpu.VMEM((2, 352, 2048), BF),
            pltpu.VMEM((2, 352, 2048), BF),
            pltpu.VMEM((352, 2048), BF),
            pltpu.VMEM((3, 32, 512), BF),
            pltpu.VMEM((4, 32, 512), BF),
            pltpu.VMEM((32, 2048), BF),
            pltpu.VMEM((2, 1024, 1152), BF),
            pltpu.VMEM((4, 32, 512), F32),
            pltpu.VMEM((2, 256, 2048), BF),
            pltpu.VMEM((256, 352), BF),
            pltpu.VMEM((4, 128, 2048), BF),
            pltpu.VMEM((4, 128, 256), BF),
            pltpu.VMEM((2, 256, 128), F32),
            pltpu.VMEM((2, 1024, 1024), BF),
            pltpu.VMEM((1024, 1024), BF),
            pltpu.VMEM((4, 2, 32, 1024), BF),
            pltpu.VMEM((4, 2, 64, 1024), BF),
            pltpu.VMEM((2, 32, 1024), BF),
            pltpu.VMEM((2, 64, 1024), BF),
            pltpu.VMEM((32, 1024), BF),
            pltpu.VMEM((4, 32, 512), BF),
            pltpu.VMEM((3, 32, 512), BF),
            pltpu.SemaphoreType.DMA((4,)),
            pltpu.SemaphoreType.DMA((MESSAGES,)),
            pltpu.SemaphoreType.DMA((MESSAGES,)),
        ],
        compiler_params=pltpu.CompilerParams(collective_id=1, has_side_effects=True, vmem_limit_bytes=60 << 20),
    )(part, hidden, gain, router_t, routes_t, live, win, wout, sin, sout)


def body(
    hidden,
    attn_gain,
    w_query,
    w_latent,
    latent_gain,
    w_key_up,
    w_value_up,
    w_out,
    kv_cache,
    lengths,
    live_mask,
    mlp_gain,
    w_router,
    routes,
    w_experts_in,
    w_experts_out,
    w_shared_in,
    w_shared_out,
):
    request_count = hidden.shape[0]
    local_heads = w_key_up.shape[0]
    cache_length = kv_cache.shape[1]
    normed = rms_norm(hidden.astype(jnp.float32), attn_gain).astype(jnp.bfloat16)
    query_all = jnp.dot(normed, w_query, preferred_element_type=jnp.float32).reshape(
        request_count, local_heads, NOPE + ROPE
    )
    positions = lengths.astype(jnp.float32)
    query_nope = query_all[..., :NOPE].astype(jnp.bfloat16)
    query_rope = rotary(query_all[..., NOPE:], positions).astype(jnp.bfloat16)
    query_latent = jnp.einsum(
        "rhn,hnc->rhc", query_nope, w_key_up, preferred_element_type=jnp.float32
    ).astype(jnp.bfloat16)
    fresh_part = jnp.dot(normed, w_latent, preferred_element_type=jnp.float32).astype(jnp.bfloat16)
    width = fresh_part.shape[1]
    gathered = head_gather(jnp.pad(fresh_part, ((0, 0), (0, 256 - width))))
    fresh_kv = jnp.concatenate([gathered[i, :, :width] for i in range(4)], axis=1)
    latent_new = rms_norm(fresh_kv[:, :LAT].astype(jnp.float32), latent_gain)
    rope_new = rotary(fresh_kv[:, LAT:].astype(jnp.float32), positions)
    key_new = jnp.concatenate([latent_new, rope_new], axis=-1).astype(jnp.bfloat16)
    query_full = jnp.concatenate([query_latent, query_rope], axis=-1)
    inverse_root = 1.0 / math.sqrt(NOPE + ROPE)
    scores = (
        jnp.einsum("rhc,rjc->rhj", query_full, kv_cache, preferred_element_type=jnp.float32)
        * inverse_root
    )
    in_cache = jnp.arange(cache_length, dtype=jnp.int32)[None, :] < lengths[:, None]
    scores = jnp.where(in_cache[:, None, :], scores, -jnp.inf)
    score_new = (
        jnp.einsum("rhc,rc->rh", query_full, key_new, preferred_element_type=jnp.float32)
        * inverse_root
    )
    highest = jnp.maximum(jnp.max(scores, axis=-1), score_new)
    weights_cached = jnp.exp(scores - highest[..., None])
    weight_new = jnp.exp(score_new - highest)
    denominator = jnp.sum(weights_cached, axis=-1) + weight_new
    probabilities = (weights_cached / denominator[..., None]).astype(jnp.bfloat16)
    prob_new = (weight_new / denominator).astype(jnp.bfloat16)
    context = jnp.einsum(
        "rhj,rjc->rhc", probabilities, kv_cache[..., :LAT], preferred_element_type=jnp.float32
    )
    context = (
        context
        + prob_new.astype(jnp.float32)[..., None] * key_new[:, None, :LAT].astype(jnp.float32)
    ).astype(jnp.bfloat16)
    values = jnp.einsum(
        "rhc,hcv->rhv", context, w_value_up, preferred_element_type=jnp.float32
    ).astype(jnp.bfloat16)
    partial_value = jnp.dot(
        values.reshape(request_count, local_heads * VDIM), w_out, preferred_element_type=jnp.float32
    ).astype(jnp.bfloat16)
    experts_in = jnp.transpose(w_experts_in, (0, 2, 3, 1)).reshape(4, 352, 2048)
    shared_in = jnp.transpose(w_shared_in, (1, 2, 0))
    return moe(
        partial_value,
        hidden,
        mlp_gain.reshape(1, -1),
        w_router.T,
        routes.T,
        live_mask.reshape(1, -1),
        experts_in,
        w_experts_out,
        shared_in,
        w_shared_out,
    )


def solution(mesh):
    placed = (
        P("dp", None),
        P(),
        P(None, "head"),
        P(None, "head"),
        P(),
        P("head", None, None),
        P("head", None, None),
        P("head", None),
        P("dp", None, None),
        P("dp"),
        P("dp"),
        P(),
        P(),
        P("dp", None),
        P("dp", None, None, "head"),
        P("dp", "head", None),
        P(None, None, "head"),
        P("head", None),
    )
    return jax.shard_map(
        body, mesh=mesh, in_specs=placed, out_specs=P("dp", "head"), check_vma=False
    )
```

```python
import functools
import math

import jax
import jax.numpy as jnp
from jax import lax
from jax.experimental import pallas as pl
from jax.experimental.pallas import tpu as pltpu
from jax.sharding import PartitionSpec as P

NOPE = 128
ROPE = 64
VDIM = 128
LAT = 512

norm_eps = 1e-06
rope_theta = 50000.0
route_scale = 2.446

MESH = pl.DeviceIdType.MESH
BF = jnp.bfloat16
F32 = jnp.float32
NT = (((1,), (1,)), ((), ()))
TN = (((0,), (0,)), ((), ()))


def rms_norm(values, weights):
    mean_square = jnp.mean(values * values, axis=-1, keepdims=True)
    return values * lax.rsqrt(mean_square + norm_eps) * weights


def rotary(values, positions):
    half_size = values.shape[-1] // 2
    frequency = rope_theta ** (-jnp.arange(half_size, dtype=jnp.float32) / half_size)
    angles = positions.reshape((-1,) + (1,) * (values.ndim - 1)) * frequency
    first_half = values[..., :half_size]
    second_half = values[..., half_size:]
    cosine = jnp.cos(angles)
    sine_part = jnp.sin(angles)
    return jnp.concatenate(
        [
            first_half * cosine - second_half * sine_part,
            second_half * cosine + first_half * sine_part,
        ],
        axis=-1,
    )


def head_gather_kernel(x_ref, o_ref, ssem, rsem):
    dp, h = lax.axis_index("dp"), lax.axis_index("head")
    barrier = pltpu.get_barrier_semaphore()
    for k in range(1, 4):
        pl.semaphore_signal(barrier, inc=1, device_id=(dp, lax.rem(h + k, 4)), device_id_type=MESH)
    pl.semaphore_wait(barrier, 3)
    copies = []
    for k in range(1, 4):
        copies.append(
            pltpu.make_async_remote_copy(
                src_ref=x_ref,
                dst_ref=o_ref.at[h],
                send_sem=ssem.at[k - 1],
                recv_sem=rsem.at[k - 1],
                device_id=(dp, lax.rem(h + k, 4)),
                device_id_type=MESH,
            )
        )
        copies[-1].start()
    o_ref[h] = x_ref[...]
    for k in range(1, 4):
        pltpu.make_async_remote_copy(
            src_ref=x_ref,
            dst_ref=o_ref.at[lax.rem(h + 4 - k, 4)],
            send_sem=ssem.at[k - 1],
            recv_sem=rsem.at[k - 1],
            device_id=(dp, lax.rem(h + k, 4)),
            device_id_type=MESH,
        ).wait()


def head_gather(x):
    return pl.pallas_call(
        head_gather_kernel,
        out_shape=jax.ShapeDtypeStruct((4,) + x.shape, x.dtype),
        in_specs=[pl.BlockSpec(memory_space=pltpu.VMEM)],
        out_specs=pl.BlockSpec(memory_space=pltpu.VMEM),
        scratch_shapes=[pltpu.SemaphoreType.DMA((3,)), pltpu.SemaphoreType.DMA((3,))],
        compiler_params=pltpu.CompilerParams(collective_id=0, has_side_effects=True),
    )(x)


def moe_kernel(
    ctx_ref, hid_ref, gain_ref, rt_ref, routes_ref, live_ref, wvu_hbm, wo_hbm, win_hbm, wout_hbm, sin_hbm, sout_hbm,
    out_ref,
    wvu, wo, part, win, wout, sin, sout, yrs, mix, ffn, xb, shared, gate_s, xs, hid_slot, outs, pmat, wslot, cb, pr, rl, rf,
    al, af, fr, yr,
    wsem, ssem, rsem, fsem,
):
    dp, h = lax.axis_index("dp"), lax.axis_index("head")
    core = lax.rem(dp, 2)
    x = lax.rem(dp // 2, 4)
    z = dp // 8
    a = x + core * (z - x)
    b = z + core * (x - z)
    sa, sb = 2 + 6 * core, 8 - 6 * core
    na, nb = 1 + 3 * core, 4 - 3 * core

    def dev(da, db):
        return (lax.rem(a + da + 4, 4) * sa + lax.rem(b + db + 4, 4) * sb + core, h)

    def num(da, db):
        return lax.rem(a + da + 4, 4) * na + lax.rem(b + db + 4, 4) * nb

    partner = (dp + 1 - 2 * core, h)

    def ypeer(k):
        return (dp, lax.rem(h + k, 4))

    weights = [
        pltpu.make_async_copy(s, d, wsem.at[i])
        for i, (s, d) in enumerate(
            (
                (sin_hbm, sin),
                (sout_hbm, sout),
                (win_hbm, win),
                (wout_hbm, wout),
            )
        )
    ]
    first_weights = [pltpu.make_async_copy(wvu_hbm, wvu, wsem.at[4]), pltpu.make_async_copy(wo_hbm, wo, wsem.at[5])]
    for copy in first_weights + weights:
        copy.start()

    barrier = pltpu.get_barrier_semaphore()
    other_dp = dp + 1 - 2 * core
    diagonal = tuple((other_dp, lax.rem(h + k, 4)) for k in range(1, 4))
    for peer in (ypeer(1), ypeer(2), ypeer(3), dev(1, 0), dev(-1, 0), dev(0, 1), dev(0, -1), partner) + diagonal:
        pl.semaphore_signal(barrier, inc=1, device_id=peer, device_id_type=MESH)
    first_weights[0].wait()
    values = jnp.concatenate(
        [jnp.dot(ctx_ref[i], wvu[i], preferred_element_type=F32).astype(BF) for i in range(4)], axis=1
    )
    first_weights[1].wait()
    for i in range(4):
        part[i] = jnp.dot(values, wo[:, i * 512 : (i + 1) * 512], preferred_element_type=F32).astype(BF)
    pl.semaphore_wait(barrier, 11)

    pending = []

    def send(i, src, dst, peer):
        copy = pltpu.make_async_remote_copy(
            src_ref=src, dst_ref=dst, send_sem=ssem.at[i], recv_sem=rsem.at[i], device_id=peer, device_id_type=MESH
        )
        copy.start()
        pending.append(copy)

    def recv(i, dst):
        pltpu.make_async_remote_copy(
            src_ref=dst, dst_ref=dst, send_sem=ssem.at[i], recv_sem=rsem.at[i], device_id=partner, device_id_type=MESH
        ).wait_recv()

    for k in range(1, 4):
        send(k - 1, part.at[lax.rem(h + k, 4)], yrs.at[k - 1], ypeer(k))
    own = pl.ds(pl.multiple_of(h * 512, 512), 512)
    attention = part[h].astype(F32)
    for k in range(1, 4):
        recv(k - 1, yrs.at[k - 1])
        attention = attention + yrs[k - 1].astype(F32)
    mix[h] = (hid_ref[:, own].astype(F32) + attention).astype(BF)
    for k in range(1, 4):
        send(2 + k, mix.at[h], mix.at[h], ypeer(k))
    for k in range(1, 4):
        recv(2 + k, mix.at[lax.rem(h + 4 - k, 4)])
    square = jnp.zeros((32, 1), F32)
    for i in range(4):
        v = mix[i].astype(F32)
        square = square + jnp.sum(v * v, axis=1, keepdims=True)
    scale = lax.rsqrt(square * (1.0 / 2048.0) + norm_eps)
    for i in range(4):
        v = mix[i].astype(F32)
        ffn[:, i * 512 : (i + 1) * 512] = (v * scale * gain_ref[:, i * 512 : (i + 1) * 512]).astype(BF)

    logits = lax.dot_general(rt_ref[...], ffn[...], NT, preferred_element_type=F32)
    expert_id = lax.broadcasted_iota(jnp.int32, (64, 32), 0)
    named = expert_id == routes_ref[0:1, :]
    for k in range(1, 6):
        named = named | (expert_id == routes_ref[k : k + 1, :])
    chosen = jnp.where(named, jax.nn.sigmoid(logits), 0.0)
    weight = route_scale * live_ref[...].astype(F32) * chosen / jnp.sum(chosen, axis=0, keepdims=True)
    w_hi = weight.astype(BF)
    w_lo = (weight - w_hi.astype(F32)).astype(BF)
    eye = (lax.broadcasted_iota(jnp.int32, (32, 32), 0) == lax.broadcasted_iota(jnp.int32, (32, 32), 1)).astype(F32).astype(BF)
    extra = lax.dot_general(eye, jnp.concatenate([w_hi, w_lo], axis=0), NT, preferred_element_type=F32).astype(BF)

    me = num(0, 0)
    rows = pl.ds(pl.multiple_of(me * 64 + core * 32, 32), 32)
    for half in range(2):
        xb[half, rows, 0:1024] = ffn[:, half * 1024 : (half + 1) * 1024]
        xb[half, rows, 1024:1152] = extra

    def block(n, low=0, count=64):
        return xb.at[core, pl.ds(pl.multiple_of(n * 64 + low, 32), count), :]

    def other(n):
        return xb.at[1 - core, pl.ds(pl.multiple_of(n * 64, 32), 64), :]

    G = 8
    PT = G + 20
    send(PT, xb.at[1 - core, rows, :], xb.at[1 - core, rows, :], partner)
    send(PT + 1, xb.at[core, rows, :], xb.at[core, rows, :], partner)
    prow = pl.ds(pl.multiple_of(me * 64 + (1 - core) * 32, 32), 32)
    recv(PT, xb.at[core, prow, :])

    order = (0, -1, 1, 2)

    def spread(j):
        base = G + 4 + 4 * j
        send(base, block(num(order[j], 0)), block(num(order[j], 0)), dev(0, 1))
        send(base + 1, block(num(order[j], 0)), block(num(order[j], 0)), dev(0, -1))

    def to_partner(j, o):
        if (j, o) != (0, 0):
            n = num(order[j], order[o])
            send(PT + 1 + 4 * j + o, block(n), block(n), partner)

    send(G, block(me), block(me), dev(1, 0))
    send(G + 1, block(me), block(me), dev(-1, 0))
    spread(0)

    weights[0].wait()
    weights[1].wait()

    def shared_gate():
        gate_s[...] = lax.dot_general(ffn[...], sin[0], NT, preferred_element_type=F32)

    def shared_up():
        gate = gate_s[...]
        up = lax.dot_general(ffn[...], sin[1], NT, preferred_element_type=F32)
        hid_slot[0:32, :] = (gate / (1.0 + jnp.exp(-gate)) * up).astype(BF)

    def shared_down(i):
        shared[i] = jnp.dot(
            hid_slot[0:32, :], sout[:, i * 512 : (i + 1) * 512], preferred_element_type=F32
        ).astype(BF)

    shared_gate()
    recv(G, block(num(-1, 0)))
    n = num(-1, 0)
    send(G + 2, block(n, 0, 32), block(n, 0, 32), dev(1, 0))
    spread(1)
    recv(G + 1, block(num(1, 0)))
    n = num(1, 0)
    send(G + 3, block(n, 32, 32), block(n, 32, 32), dev(-1, 0))
    spread(2)
    shared_up()

    def first(j):
        base = G + 4 + 4 * j
        n = num(order[j], -1)
        recv(base, block(n))
        send(base + 2, block(n, 0, 32), block(n, 0, 32), dev(0, 1))
        n = num(order[j], 1)
        recv(base + 1, block(n))
        send(base + 3, block(n, 32, 32), block(n, 32, 32), dev(0, -1))
        to_partner(j, 1)
        to_partner(j, 2)

    def second(j):
        base = G + 4 + 4 * j
        n = num(order[j], 2)
        recv(base + 2, block(n, 0, 32))
        recv(base + 3, block(n, 32, 32))
        to_partner(j, 3)

    first(0)
    recv(G + 2, block(num(2, 0), 0, 32))
    recv(G + 3, block(num(2, 0), 32, 32))
    spread(3)
    for j in range(1, 4):
        to_partner(j, 0)
    shared_down(0)
    first(1)
    shared_down(1)
    first(2)
    shared_down(2)
    second(0)
    shared_down(3)
    first(3)
    F = PT + 17 + 4 + 20
    for k in range(1, 4):
        send(F + k, shared.at[lax.rem(h + k, 4)], yr.at[k - 1], ypeer(k))
    second(1)
    second(2)
    second(3)

    prow2 = pl.ds(pl.multiple_of(me * 64 + (1 - core) * 32, 32), 32)
    recv(PT + 1, xb.at[1 - core, prow2, :])
    for j in range(4):
        for o in range(4):
            if (j, o) != (0, 0):
                recv(PT + 1 + 4 * j + o, other(num(order[o], order[j])))

    lane = lax.broadcasted_iota(jnp.int32, (8, 128), 1)
    row = lax.broadcasted_iota(jnp.int32, (8, 128), 0)
    target = 2 * dp + lax.rem(row, 2) + 64 * (row // 2)
    pick = jnp.where((lane == target) & (row < 4), 1.0, 0.0).astype(BF)
    t_from = lax.broadcasted_iota(jnp.int32, (256, 256), 0)
    t_to = lax.broadcasted_iota(jnp.int32, (256, 256), 1)
    before = jnp.where((t_from < t_to) & (t_from // 32 == t_to // 32), 1.0, 0.0).astype(BF)
    source = lax.broadcasted_iota(jnp.int32, (1, 256), 1) // 32
    slot = lax.broadcasted_iota(jnp.int32, (64, 256), 0)
    for g in range(4):
        info = lax.dot_general(pick, xb[0, g * 256 : (g + 1) * 256, 1024:1152], NT, preferred_element_type=F32)
        mask = jnp.where(info != 0.0, 1.0, 0.0)
        rank = jnp.dot(mask.astype(BF), before, preferred_element_type=F32)
        for e in range(2):
            value = info[e : e + 1, :] + info[2 + e : 3 + e, :]
            place = jnp.where(mask[e : e + 1, :] > 0.0, 8 * source + rank[e : e + 1, :].astype(jnp.int32), -1)
            hit = jnp.where(slot == place, 1.0, 0.0)
            wslot[e, g * 64 : (g + 1) * 64, :] = jnp.broadcast_to(
                jnp.sum(hit * value, axis=1, keepdims=True), (64, 128)
            )
            hit = hit.astype(BF)
            pmat[g, e * 64 : (e + 1) * 64, :] = hit
        for half in range(2):
            got = jnp.dot(
                pmat[g], xb[half, g * 256 : (g + 1) * 256, 0:1024], preferred_element_type=F32
            ).astype(BF)
            for e in range(2):
                xs[e, g * 64 : (g + 1) * 64, half * 1024 : (half + 1) * 1024] = got[e * 64 : (e + 1) * 64]

    weights[2].wait()
    weights[3].wait()
    for e in range(2):
        gate = lax.dot_general(xs[e], win[2 * e], NT, preferred_element_type=F32)
        up = lax.dot_general(xs[e], win[2 * e + 1], NT, preferred_element_type=F32)
        hid_slot[...] = (gate / (1.0 + jnp.exp(-gate)) * up).astype(BF)
        for i in range(4):
            result = jnp.dot(hid_slot[...], wout[e, :, i * 512 : (i + 1) * 512], preferred_element_type=F32)
            result = (result * wslot[e, :, 0:1]).astype(BF)
            for g in range(4):
                outs[g, e * 64 : (e + 1) * 64, i * 512 : (i + 1) * 512] = result[g * 64 : (g + 1) * 64]

    R = PT + 17
    for g in range(4):
        for half in range(2):
            cb[half, g * 256 : (g + 1) * 256, :] = lax.dot_general(
                pmat[g], outs[g, :, half * 1024 : (half + 1) * 1024], TN, preferred_element_type=F32
            ).astype(BF)
        span = pl.ds(g * 256, 256)
        send(R + g, cb.at[1 - core, span, :], pr.at[span, :], partner)
    for g in range(4):
        span = pl.ds(g * 256, 256)
        recv(R + g, pr.at[span, :])
        cb[core, span, :] = (cb[core, span, :].astype(F32) + pr[span, :].astype(F32)).astype(BF)

    def cpart(n, low=0, count=64):
        return pl.ds(pl.multiple_of(n * 64 + low, 32), count)

    def ring(base, here, ahead, behind, far, up_dev, down_dev, lows, fulls, stage):
        if stage == 0:
            send(base, cb.at[core, cpart(far, 0, 32), :], lows.at[0], up_dev)
            send(base + 1, cb.at[core, cpart(far, 32, 32), :], lows.at[1], down_dev)
        elif stage == 1:
            recv(base, lows.at[0])
            s = cpart(ahead, 0, 32)
            cb[core, s, :] = (cb[core, s, :].astype(F32) + lows[0].astype(F32)).astype(BF)
            send(base + 2, cb.at[core, cpart(ahead), :], fulls.at[0], up_dev)
            recv(base + 1, lows.at[1])
            s = cpart(behind, 32, 32)
            cb[core, s, :] = (cb[core, s, :].astype(F32) + lows[1].astype(F32)).astype(BF)
            send(base + 3, cb.at[core, cpart(behind), :], fulls.at[1], down_dev)
        else:
            recv(base + 2, fulls.at[0])
            recv(base + 3, fulls.at[1])
            s = cpart(here)
            cb[core, s, :] = (cb[core, s, :].astype(F32) + fulls[0].astype(F32) + fulls[1].astype(F32)).astype(BF)

    S = R + 4
    back = (2, 1, -1, 0)

    def bring(j, stage):
        d = back[j]
        ring(S + 4 * j, num(d, 0), num(d, 1), num(d, -1), num(d, 2), dev(0, 1), dev(0, -1), rl.at[j], rf.at[j], stage)

    def aring(stage):
        ring(S + 16, num(0, 0), num(1, 0), num(-1, 0), num(2, 0), dev(1, 0), dev(-1, 0), al, af, stage)

    for j in range(4):
        bring(j, 0)
    for j in range(4):
        bring(j, 1)
    bring(0, 2)
    aring(0)
    bring(1, 2)
    bring(2, 2)
    aring(1)
    bring(3, 2)
    aring(2)

    local = []
    for q in range(2):
        owner = 2 * core + q
        for t, (span, where) in enumerate(((rows, dp), (prow, other_dp))):
            copy = pltpu.make_async_remote_copy(
                src_ref=cb.at[core, span, pl.ds(q * 512, 512)],
                dst_ref=fr.at[h],
                send_sem=fsem.at[2 * q + t],
                recv_sem=fsem.at[4 + h],
                device_id=(where, owner),
                device_id_type=MESH,
            )
            if t == 1:
                copy.start()
                pending.append(copy)
            else:
                pl.when(owner != h)(copy.start)
                local.append((owner, copy))
    result = mix[h].astype(F32) + shared[h].astype(F32)
    for k in range(1, 4):
        recv(F + k, yr.at[k - 1])
        result = result + yr[k - 1].astype(F32)

    def routed_recv(o):
        pltpu.make_async_remote_copy(
            src_ref=fr.at[o],
            dst_ref=fr.at[o],
            send_sem=fsem.at[0],
            recv_sem=fsem.at[4 + o],
            device_id=partner,
            device_id_type=MESH,
        ).wait_recv()

    mine = core == h // 2

    @pl.when(mine)
    def _():
        fr[h] = cb[core, rows, pl.ds(pl.multiple_of(lax.rem(h, 2) * 512, 512), 512)]

    @pl.when(jnp.logical_not(mine))
    def _():
        routed_recv(h)

    for k in range(1, 4):
        routed_recv(lax.rem(h + k, 4))
    for i in range(4):
        result = result + fr[i].astype(F32)
    out_ref[...] = result.astype(BF)
    for copy in pending:
        copy.wait_send()
    for owner, copy in local:
        pl.when(owner != h)(copy.wait_send)


MESSAGES = 8 + 20 + 17 + 4 + 20 + 4


def moe(context, hidden, gain, router_t, routes_t, live, wvu, wo, win, wout, sin, sout):
    vmem = pl.BlockSpec(memory_space=pltpu.VMEM)
    hbm = pl.BlockSpec(memory_space=pl.ANY)
    return pl.pallas_call(
        moe_kernel,
        out_shape=jax.ShapeDtypeStruct((32, 512), BF),
        in_specs=[vmem] * 6 + [hbm] * 6,
        out_specs=vmem,
        scratch_shapes=[
            pltpu.VMEM((4, 512, 128), BF),
            pltpu.VMEM((512, 2048), BF),
            pltpu.VMEM((4, 32, 512), BF),
            pltpu.VMEM((4, 352, 2048), BF),
            pltpu.VMEM((2, 352, 2048), BF),
            pltpu.VMEM((2, 352, 2048), BF),
            pltpu.VMEM((352, 2048), BF),
            pltpu.VMEM((3, 32, 512), BF),
            pltpu.VMEM((4, 32, 512), BF),
            pltpu.VMEM((32, 2048), BF),
            pltpu.VMEM((2, 1024, 1152), BF),
            pltpu.VMEM((4, 32, 512), BF),
            pltpu.VMEM((32, 352), F32),
            pltpu.VMEM((2, 256, 2048), BF),
            pltpu.VMEM((256, 352), BF),
            pltpu.VMEM((4, 128, 2048), BF),
            pltpu.VMEM((4, 128, 256), BF),
            pltpu.VMEM((2, 256, 128), F32),
            pltpu.VMEM((2, 1024, 1024), BF),
            pltpu.VMEM((1024, 1024), BF),
            pltpu.VMEM((4, 2, 32, 1024), BF),
            pltpu.VMEM((4, 2, 64, 1024), BF),
            pltpu.VMEM((2, 32, 1024), BF),
            pltpu.VMEM((2, 64, 1024), BF),
            pltpu.VMEM((4, 32, 512), BF),
            pltpu.VMEM((3, 32, 512), BF),
            pltpu.SemaphoreType.DMA((6,)),
            pltpu.SemaphoreType.DMA((MESSAGES,)),
            pltpu.SemaphoreType.DMA((MESSAGES,)),
            pltpu.SemaphoreType.DMA((8,)),
        ],
        compiler_params=pltpu.CompilerParams(collective_id=1, has_side_effects=True, vmem_limit_bytes=60 << 20),
    )(context, hidden, gain, router_t, routes_t, live, wvu, wo, win, wout, sin, sout)


def body(
    hidden,
    attn_gain,
    w_query,
    w_latent,
    latent_gain,
    w_key_up,
    w_value_up,
    w_out,
    kv_cache,
    lengths,
    live_mask,
    mlp_gain,
    w_router,
    routes,
    w_experts_in,
    w_experts_out,
    w_shared_in,
    w_shared_out,
):
    request_count = hidden.shape[0]
    local_heads = w_key_up.shape[0]
    cache_length = kv_cache.shape[1]
    normed = rms_norm(hidden.astype(jnp.float32), attn_gain).astype(jnp.bfloat16)
    query_all = jnp.dot(normed, w_query, preferred_element_type=jnp.float32).reshape(
        request_count, local_heads, NOPE + ROPE
    )
    positions = lengths.astype(jnp.float32)
    query_nope = query_all[..., :NOPE].astype(jnp.bfloat16)
    query_rope = rotary(query_all[..., NOPE:], positions).astype(jnp.bfloat16)
    query_latent = jnp.einsum(
        "rhn,hnc->rhc", query_nope, w_key_up, preferred_element_type=jnp.float32
    ).astype(jnp.bfloat16)
    fresh_part = jnp.dot(normed, w_latent, preferred_element_type=jnp.float32).astype(jnp.bfloat16)
    width = fresh_part.shape[1]
    gathered = head_gather(jnp.pad(fresh_part, ((0, 0), (0, 256 - width))))
    fresh_kv = jnp.concatenate([gathered[i, :, :width] for i in range(4)], axis=1)
    latent_new = rms_norm(fresh_kv[:, :LAT].astype(jnp.float32), latent_gain)
    rope_new = rotary(fresh_kv[:, LAT:].astype(jnp.float32), positions)
    key_new = jnp.concatenate([latent_new, rope_new], axis=-1).astype(jnp.bfloat16)
    query_full = jnp.concatenate([query_latent, query_rope], axis=-1)
    inverse_root = 1.0 / math.sqrt(NOPE + ROPE)
    scores = (
        jnp.einsum("rhc,rjc->rhj", query_full, kv_cache, preferred_element_type=jnp.float32)
        * inverse_root
    )
    in_cache = jnp.arange(cache_length, dtype=jnp.int32)[None, :] < lengths[:, None]
    scores = jnp.where(in_cache[:, None, :], scores, -jnp.inf)
    score_new = (
        jnp.einsum("rhc,rc->rh", query_full, key_new, preferred_element_type=jnp.float32)
        * inverse_root
    )
    highest = jnp.maximum(jnp.max(scores, axis=-1), score_new)
    weights_cached = jnp.exp(scores - highest[..., None])
    weight_new = jnp.exp(score_new - highest)
    denominator = jnp.sum(weights_cached, axis=-1) + weight_new
    probabilities = (weights_cached / denominator[..., None]).astype(jnp.bfloat16)
    prob_new = (weight_new / denominator).astype(jnp.bfloat16)
    context = jnp.einsum(
        "rhj,rjc->rhc", probabilities, kv_cache[..., :LAT], preferred_element_type=jnp.float32
    )
    context = (
        context
        + prob_new.astype(jnp.float32)[..., None] * key_new[:, None, :LAT].astype(jnp.float32)
    ).astype(jnp.bfloat16)
    experts_in = jnp.transpose(w_experts_in, (0, 2, 3, 1)).reshape(4, 352, 2048)
    shared_in = jnp.transpose(w_shared_in, (1, 2, 0))
    return moe(
        jnp.transpose(context, (1, 0, 2)),
        hidden,
        mlp_gain.reshape(1, -1),
        w_router.T,
        routes.T,
        live_mask.reshape(1, -1),
        w_value_up,
        w_out,
        experts_in,
        w_experts_out,
        shared_in,
        w_shared_out,
    )


def solution(mesh):
    placed = (
        P("dp", None),
        P(),
        P(None, "head"),
        P(None, "head"),
        P(),
        P("head", None, None),
        P("head", None, None),
        P("head", None),
        P("dp", None, None),
        P("dp"),
        P("dp"),
        P(),
        P(),
        P("dp", None),
        P("dp", None, None, "head"),
        P("dp", "head", None),
        P(None, None, "head"),
        P("head", None),
    )
    return jax.shard_map(
        body, mesh=mesh, in_specs=placed, out_specs=P("dp", "head"), check_vma=False
    )
```

```python
import functools
import math

import jax
import jax.numpy as jnp
from jax import lax
from jax.experimental import pallas as pl
from jax.experimental.pallas import tpu as pltpu
from jax.sharding import PartitionSpec as P

NOPE = 128
ROPE = 64
VDIM = 128
LAT = 512

norm_eps = 1e-06
rope_theta = 50000.0
route_scale = 2.446

MESH = pl.DeviceIdType.MESH
BF = jnp.bfloat16
F32 = jnp.float32
NT = (((1,), (1,)), ((), ()))
TN = (((0,), (0,)), ((), ()))


def rms_norm(values, weights):
    mean_square = jnp.mean(values * values, axis=-1, keepdims=True)
    return values * lax.rsqrt(mean_square + norm_eps) * weights


def rotary(values, positions):
    half_size = values.shape[-1] // 2
    frequency = rope_theta ** (-jnp.arange(half_size, dtype=jnp.float32) / half_size)
    angles = positions.reshape((-1,) + (1,) * (values.ndim - 1)) * frequency
    first_half = values[..., :half_size]
    second_half = values[..., half_size:]
    cosine = jnp.cos(angles)
    sine_part = jnp.sin(angles)
    return jnp.concatenate(
        [
            first_half * cosine - second_half * sine_part,
            second_half * cosine + first_half * sine_part,
        ],
        axis=-1,
    )


def front_kernel(hid_ref, gain_ref, wlat_ref, wq_hbm, o_ref, q_ref, wq, fresh, wsem, ssem, rsem):
    dp, h = lax.axis_index("dp"), lax.axis_index("head")
    weight = pltpu.make_async_copy(wq_hbm, wq, wsem)
    weight.start()
    barrier = pltpu.get_barrier_semaphore()
    for k in range(1, 4):
        pl.semaphore_signal(barrier, inc=1, device_id=(dp, lax.rem(h + k, 4)), device_id_type=MESH)
    normed = rms_norm(hid_ref[...].astype(F32), gain_ref[...]).astype(BF)
    width = wlat_ref.shape[0]
    fresh[...] = jnp.zeros_like(fresh)
    fresh[:, 0:width] = lax.dot_general(normed, wlat_ref[...], NT, preferred_element_type=F32).astype(BF)
    pl.semaphore_wait(barrier, 3)
    for k in range(1, 4):
        pltpu.make_async_remote_copy(
            src_ref=fresh,
            dst_ref=o_ref.at[h],
            send_sem=ssem.at[k - 1],
            recv_sem=rsem.at[k - 1],
            device_id=(dp, lax.rem(h + k, 4)),
            device_id_type=MESH,
        ).start()
    o_ref[h] = fresh[...]
    weight.wait()
    q_ref[...] = jnp.dot(normed, wq[...], preferred_element_type=F32)
    for k in range(1, 4):
        pltpu.make_async_remote_copy(
            src_ref=fresh,
            dst_ref=o_ref.at[lax.rem(h + 4 - k, 4)],
            send_sem=ssem.at[k - 1],
            recv_sem=rsem.at[k - 1],
            device_id=(dp, lax.rem(h + k, 4)),
            device_id_type=MESH,
        ).wait()


def front(hidden, gain, w_latent_t, w_query):
    vmem = pl.BlockSpec(memory_space=pltpu.VMEM)
    rows = hidden.shape[0]
    return pl.pallas_call(
        front_kernel,
        out_shape=(
            jax.ShapeDtypeStruct((4, rows, 256), BF),
            jax.ShapeDtypeStruct((rows, w_query.shape[1]), F32),
        ),
        in_specs=[vmem, vmem, vmem, pl.BlockSpec(memory_space=pl.ANY)],
        out_specs=(vmem, vmem),
        scratch_shapes=[
            pltpu.VMEM(w_query.shape, BF),
            pltpu.VMEM((rows, 256), BF),
            pltpu.SemaphoreType.DMA,
            pltpu.SemaphoreType.DMA((3,)),
            pltpu.SemaphoreType.DMA((3,)),
        ],
        compiler_params=pltpu.CompilerParams(collective_id=0, has_side_effects=True, vmem_limit_bytes=24 << 20),
    )(hidden, gain, w_latent_t, w_query)


def moe_kernel(
    val_ref, hid_ref, gain_ref, rt_ref, routes_ref, live_ref, wo_hbm, win_hbm, wout_hbm, sin_hbm, sout_hbm,
    out_ref,
    wo, part, win, wout, sin, sout, yrs, mix, ffn, xb, shared, gate_s, xs, hid_slot, outs, pmat, wslot, cb, pr, rl, rf,
    al, af, fr, yr,
    wsem, ssem, rsem, fsem,
):
    dp, h = lax.axis_index("dp"), lax.axis_index("head")
    core = lax.rem(dp, 2)
    x = lax.rem(dp // 2, 4)
    z = dp // 8
    a = x + core * (z - x)
    b = z + core * (x - z)
    sa, sb = 2 + 6 * core, 8 - 6 * core
    na, nb = 1 + 3 * core, 4 - 3 * core

    def dev(da, db):
        return (lax.rem(a + da + 4, 4) * sa + lax.rem(b + db + 4, 4) * sb + core, h)

    def num(da, db):
        return lax.rem(a + da + 4, 4) * na + lax.rem(b + db + 4, 4) * nb

    partner = (dp + 1 - 2 * core, h)

    def ypeer(k):
        return (dp, lax.rem(h + k, 4))

    weights = [
        pltpu.make_async_copy(s, d, wsem.at[i])
        for i, (s, d) in enumerate(
            (
                (sin_hbm, sin),
                (sout_hbm, sout),
                (win_hbm, win),
                (wout_hbm, wout),
            )
        )
    ]
    out_weight = pltpu.make_async_copy(wo_hbm, wo, wsem.at[4])
    for copy in [out_weight] + weights:
        copy.start()

    barrier = pltpu.get_barrier_semaphore()
    other_dp = dp + 1 - 2 * core
    diagonal = tuple((other_dp, lax.rem(h + k, 4)) for k in range(1, 4))
    for peer in (ypeer(1), ypeer(2), ypeer(3), dev(1, 0), dev(-1, 0), dev(0, 1), dev(0, -1), partner) + diagonal:
        pl.semaphore_signal(barrier, inc=1, device_id=peer, device_id_type=MESH)
    out_weight.wait()
    for i in range(4):
        part[i] = jnp.dot(val_ref[...], wo[:, i * 512 : (i + 1) * 512], preferred_element_type=F32).astype(BF)
    pl.semaphore_wait(barrier, 11)

    pending = []

    def send(i, src, dst, peer):
        copy = pltpu.make_async_remote_copy(
            src_ref=src, dst_ref=dst, send_sem=ssem.at[i], recv_sem=rsem.at[i], device_id=peer, device_id_type=MESH
        )
        copy.start()
        pending.append(copy)

    def recv(i, dst):
        pltpu.make_async_remote_copy(
            src_ref=dst, dst_ref=dst, send_sem=ssem.at[i], recv_sem=rsem.at[i], device_id=partner, device_id_type=MESH
        ).wait_recv()

    for k in range(1, 4):
        send(k - 1, part.at[lax.rem(h + k, 4)], yrs.at[k - 1], ypeer(k))
    own = pl.ds(pl.multiple_of(h * 512, 512), 512)
    attention = part[h].astype(F32)
    for k in range(1, 4):
        recv(k - 1, yrs.at[k - 1])
        attention = attention + yrs[k - 1].astype(F32)
    mix[h] = (hid_ref[:, own].astype(F32) + attention).astype(BF)
    for k in range(1, 4):
        send(2 + k, mix.at[h], mix.at[h], ypeer(k))
    for k in range(1, 4):
        recv(2 + k, mix.at[lax.rem(h + 4 - k, 4)])
    square = jnp.zeros((32, 1), F32)
    for i in range(4):
        v = mix[i].astype(F32)
        square = square + jnp.sum(v * v, axis=1, keepdims=True)
    scale = lax.rsqrt(square * (1.0 / 2048.0) + norm_eps)
    for i in range(4):
        v = mix[i].astype(F32)
        ffn[:, i * 512 : (i + 1) * 512] = (v * scale * gain_ref[:, i * 512 : (i + 1) * 512]).astype(BF)

    logits = lax.dot_general(rt_ref[...], ffn[...], NT, preferred_element_type=F32)
    expert_id = lax.broadcasted_iota(jnp.int32, (64, 32), 0)
    named = expert_id == routes_ref[0:1, :]
    for k in range(1, 6):
        named = named | (expert_id == routes_ref[k : k + 1, :])
    chosen = jnp.where(named, jax.nn.sigmoid(logits), 0.0)
    weight = route_scale * live_ref[...].astype(F32) * chosen / jnp.sum(chosen, axis=0, keepdims=True)
    w_hi = weight.astype(BF)
    w_lo = (weight - w_hi.astype(F32)).astype(BF)
    eye = (lax.broadcasted_iota(jnp.int32, (32, 32), 0) == lax.broadcasted_iota(jnp.int32, (32, 32), 1)).astype(F32).astype(BF)
    extra = lax.dot_general(eye, jnp.concatenate([w_hi, w_lo], axis=0), NT, preferred_element_type=F32).astype(BF)

    me = num(0, 0)
    rows = pl.ds(pl.multiple_of(me * 64 + core * 32, 32), 32)
    for half in range(2):
        xb[half, rows, 0:1024] = ffn[:, half * 1024 : (half + 1) * 1024]
        xb[half, rows, 1024:1152] = extra

    def block(n, low=0, count=64):
        return xb.at[core, pl.ds(pl.multiple_of(n * 64 + low, 32), count), :]

    def other(n):
        return xb.at[1 - core, pl.ds(pl.multiple_of(n * 64, 32), 64), :]

    G = 8
    PT = G + 20
    send(PT, xb.at[1 - core, rows, :], xb.at[1 - core, rows, :], partner)
    send(PT + 1, xb.at[core, rows, :], xb.at[core, rows, :], partner)
    prow = pl.ds(pl.multiple_of(me * 64 + (1 - core) * 32, 32), 32)
    recv(PT, xb.at[core, prow, :])

    order = (0, -1, 1, 2)

    def spread(j):
        base = G + 4 + 4 * j
        send(base, block(num(order[j], 0)), block(num(order[j], 0)), dev(0, 1))
        send(base + 1, block(num(order[j], 0)), block(num(order[j], 0)), dev(0, -1))

    def to_partner(j, o):
        if (j, o) != (0, 0):
            n = num(order[j], order[o])
            send(PT + 1 + 4 * j + o, block(n), block(n), partner)

    send(G, block(me), block(me), dev(1, 0))
    send(G + 1, block(me), block(me), dev(-1, 0))
    spread(0)

    weights[0].wait()
    weights[1].wait()

    def shared_gate():
        gate_s[...] = lax.dot_general(ffn[...], sin[0], NT, preferred_element_type=F32)

    def shared_up():
        gate = gate_s[...]
        up = lax.dot_general(ffn[...], sin[1], NT, preferred_element_type=F32)
        hid_slot[0:32, :] = (gate / (1.0 + jnp.exp(-gate)) * up).astype(BF)

    def shared_down(i):
        shared[i] = jnp.dot(
            hid_slot[0:32, :], sout[:, i * 512 : (i + 1) * 512], preferred_element_type=F32
        ).astype(BF)

    shared_gate()
    recv(G, block(num(-1, 0)))
    n = num(-1, 0)
    send(G + 2, block(n, 0, 32), block(n, 0, 32), dev(1, 0))
    spread(1)
    recv(G + 1, block(num(1, 0)))
    n = num(1, 0)
    send(G + 3, block(n, 32, 32), block(n, 32, 32), dev(-1, 0))
    spread(2)
    shared_up()

    def first(j):
        base = G + 4 + 4 * j
        n = num(order[j], -1)
        recv(base, block(n))
        send(base + 2, block(n, 0, 32), block(n, 0, 32), dev(0, 1))
        n = num(order[j], 1)
        recv(base + 1, block(n))
        send(base + 3, block(n, 32, 32), block(n, 32, 32), dev(0, -1))
        to_partner(j, 1)
        to_partner(j, 2)

    def second(j):
        base = G + 4 + 4 * j
        n = num(order[j], 2)
        recv(base + 2, block(n, 0, 32))
        recv(base + 3, block(n, 32, 32))
        to_partner(j, 3)

    first(0)
    recv(G + 2, block(num(2, 0), 0, 32))
    recv(G + 3, block(num(2, 0), 32, 32))
    spread(3)
    for j in range(1, 4):
        to_partner(j, 0)
    shared_down(0)
    first(1)
    shared_down(1)
    first(2)
    shared_down(2)
    second(0)
    shared_down(3)
    first(3)
    F = PT + 17 + 4 + 20
    for k in range(1, 4):
        send(F + k, shared.at[lax.rem(h + k, 4)], yr.at[k - 1], ypeer(k))
    second(1)
    second(2)
    second(3)

    prow2 = pl.ds(pl.multiple_of(me * 64 + (1 - core) * 32, 32), 32)
    recv(PT + 1, xb.at[1 - core, prow2, :])
    for j in range(4):
        for o in range(4):
            if (j, o) != (0, 0):
                recv(PT + 1 + 4 * j + o, other(num(order[o], order[j])))

    lane = lax.broadcasted_iota(jnp.int32, (8, 128), 1)
    row = lax.broadcasted_iota(jnp.int32, (8, 128), 0)
    target = 2 * dp + lax.rem(row, 2) + 64 * (row // 2)
    pick = jnp.where((lane == target) & (row < 4), 1.0, 0.0).astype(BF)
    t_from = lax.broadcasted_iota(jnp.int32, (256, 256), 0)
    t_to = lax.broadcasted_iota(jnp.int32, (256, 256), 1)
    before = jnp.where((t_from < t_to) & (t_from // 32 == t_to // 32), 1.0, 0.0).astype(BF)
    source = lax.broadcasted_iota(jnp.int32, (1, 256), 1) // 32
    slot = lax.broadcasted_iota(jnp.int32, (64, 256), 0)
    for g in range(4):
        info = lax.dot_general(pick, xb[0, g * 256 : (g + 1) * 256, 1024:1152], NT, preferred_element_type=F32)
        mask = jnp.where(info != 0.0, 1.0, 0.0)
        rank = jnp.dot(mask.astype(BF), before, preferred_element_type=F32)
        for e in range(2):
            value = info[e : e + 1, :] + info[2 + e : 3 + e, :]
            place = jnp.where(mask[e : e + 1, :] > 0.0, 8 * source + rank[e : e + 1, :].astype(jnp.int32), -1)
            hit = jnp.where(slot == place, 1.0, 0.0)
            wslot[e, g * 64 : (g + 1) * 64, :] = jnp.broadcast_to(
                jnp.sum(hit * value, axis=1, keepdims=True), (64, 128)
            )
            hit = hit.astype(BF)
            pmat[g, e * 64 : (e + 1) * 64, :] = hit
        for half in range(2):
            got = jnp.dot(
                pmat[g], xb[half, g * 256 : (g + 1) * 256, 0:1024], preferred_element_type=F32
            ).astype(BF)
            for e in range(2):
                xs[e, g * 64 : (g + 1) * 64, half * 1024 : (half + 1) * 1024] = got[e * 64 : (e + 1) * 64]

    weights[2].wait()
    weights[3].wait()
    for e in range(2):
        gate = lax.dot_general(xs[e], win[2 * e], NT, preferred_element_type=F32)
        up = lax.dot_general(xs[e], win[2 * e + 1], NT, preferred_element_type=F32)
        hid_slot[...] = (gate / (1.0 + jnp.exp(-gate)) * up).astype(BF)
        for i in range(4):
            result = jnp.dot(hid_slot[...], wout[e, :, i * 512 : (i + 1) * 512], preferred_element_type=F32)
            result = (result * wslot[e, :, 0:1]).astype(BF)
            for g in range(4):
                outs[g, e * 64 : (e + 1) * 64, i * 512 : (i + 1) * 512] = result[g * 64 : (g + 1) * 64]

    R = PT + 17
    for g in range(4):
        for half in range(2):
            cb[half, g * 256 : (g + 1) * 256, :] = lax.dot_general(
                pmat[g], outs[g, :, half * 1024 : (half + 1) * 1024], TN, preferred_element_type=F32
            ).astype(BF)
        span = pl.ds(g * 256, 256)
        send(R + g, cb.at[1 - core, span, :], pr.at[span, :], partner)
    for g in range(4):
        span = pl.ds(g * 256, 256)
        recv(R + g, pr.at[span, :])
        cb[core, span, :] = (cb[core, span, :].astype(F32) + pr[span, :].astype(F32)).astype(BF)

    def cpart(n, low=0, count=64):
        return pl.ds(pl.multiple_of(n * 64 + low, 32), count)

    def ring(base, here, ahead, behind, far, up_dev, down_dev, lows, fulls, stage):
        if stage == 0:
            send(base, cb.at[core, cpart(far, 0, 32), :], lows.at[0], up_dev)
            send(base + 1, cb.at[core, cpart(far, 32, 32), :], lows.at[1], down_dev)
        elif stage == 1:
            recv(base, lows.at[0])
            s = cpart(ahead, 0, 32)
            cb[core, s, :] = (cb[core, s, :].astype(F32) + lows[0].astype(F32)).astype(BF)
            send(base + 2, cb.at[core, cpart(ahead), :], fulls.at[0], up_dev)
            recv(base + 1, lows.at[1])
            s = cpart(behind, 32, 32)
            cb[core, s, :] = (cb[core, s, :].astype(F32) + lows[1].astype(F32)).astype(BF)
            send(base + 3, cb.at[core, cpart(behind), :], fulls.at[1], down_dev)
        else:
            recv(base + 2, fulls.at[0])
            recv(base + 3, fulls.at[1])
            s = cpart(here)
            cb[core, s, :] = (cb[core, s, :].astype(F32) + fulls[0].astype(F32) + fulls[1].astype(F32)).astype(BF)

    S = R + 4
    back = (2, 1, -1, 0)

    def bring(j, stage):
        d = back[j]
        ring(S + 4 * j, num(d, 0), num(d, 1), num(d, -1), num(d, 2), dev(0, 1), dev(0, -1), rl.at[j], rf.at[j], stage)

    def aring(stage):
        ring(S + 16, num(0, 0), num(1, 0), num(-1, 0), num(2, 0), dev(1, 0), dev(-1, 0), al, af, stage)

    for j in range(4):
        bring(j, 0)
    for j in range(4):
        bring(j, 1)
    bring(0, 2)
    aring(0)
    bring(1, 2)
    bring(2, 2)
    aring(1)
    bring(3, 2)
    aring(2)

    local = []
    for q in range(2):
        owner = 2 * core + q
        for t, (span, where) in enumerate(((rows, dp), (prow, other_dp))):
            copy = pltpu.make_async_remote_copy(
                src_ref=cb.at[core, span, pl.ds(q * 512, 512)],
                dst_ref=fr.at[h],
                send_sem=fsem.at[2 * q + t],
                recv_sem=fsem.at[4 + h],
                device_id=(where, owner),
                device_id_type=MESH,
            )
            if t == 1:
                copy.start()
                pending.append(copy)
            else:
                pl.when(owner != h)(copy.start)
                local.append((owner, copy))
    result = mix[h].astype(F32) + shared[h].astype(F32)
    for k in range(1, 4):
        recv(F + k, yr.at[k - 1])
        result = result + yr[k - 1].astype(F32)

    def routed_recv(o):
        pltpu.make_async_remote_copy(
            src_ref=fr.at[o],
            dst_ref=fr.at[o],
            send_sem=fsem.at[0],
            recv_sem=fsem.at[4 + o],
            device_id=partner,
            device_id_type=MESH,
        ).wait_recv()

    mine = core == h // 2

    @pl.when(mine)
    def _():
        fr[h] = cb[core, rows, pl.ds(pl.multiple_of(lax.rem(h, 2) * 512, 512), 512)]

    @pl.when(jnp.logical_not(mine))
    def _():
        routed_recv(h)

    for k in range(1, 4):
        routed_recv(lax.rem(h + k, 4))
    for i in range(4):
        result = result + fr[i].astype(F32)
    out_ref[...] = result.astype(BF)
    for copy in pending:
        copy.wait_send()
    for owner, copy in local:
        pl.when(owner != h)(copy.wait_send)


MESSAGES = 8 + 20 + 17 + 4 + 20 + 4


def moe(values, hidden, gain, router_t, routes_t, live, wo, win, wout, sin, sout):
    vmem = pl.BlockSpec(memory_space=pltpu.VMEM)
    hbm = pl.BlockSpec(memory_space=pl.ANY)
    return pl.pallas_call(
        moe_kernel,
        out_shape=jax.ShapeDtypeStruct((32, 512), BF),
        in_specs=[vmem] * 6 + [hbm] * 5,
        out_specs=vmem,
        scratch_shapes=[
            pltpu.VMEM((512, 2048), BF),
            pltpu.VMEM((4, 32, 512), BF),
            pltpu.VMEM((4, 352, 2048), BF),
            pltpu.VMEM((2, 352, 2048), BF),
            pltpu.VMEM((2, 352, 2048), BF),
            pltpu.VMEM((352, 2048), BF),
            pltpu.VMEM((3, 32, 512), BF),
            pltpu.VMEM((4, 32, 512), BF),
            pltpu.VMEM((32, 2048), BF),
            pltpu.VMEM((2, 1024, 1152), BF),
            pltpu.VMEM((4, 32, 512), BF),
            pltpu.VMEM((32, 352), F32),
            pltpu.VMEM((2, 256, 2048), BF),
            pltpu.VMEM((256, 352), BF),
            pltpu.VMEM((4, 128, 2048), BF),
            pltpu.VMEM((4, 128, 256), BF),
            pltpu.VMEM((2, 256, 128), F32),
            pltpu.VMEM((2, 1024, 1024), BF),
            pltpu.VMEM((1024, 1024), BF),
            pltpu.VMEM((4, 2, 32, 1024), BF),
            pltpu.VMEM((4, 2, 64, 1024), BF),
            pltpu.VMEM((2, 32, 1024), BF),
            pltpu.VMEM((2, 64, 1024), BF),
            pltpu.VMEM((4, 32, 512), BF),
            pltpu.VMEM((3, 32, 512), BF),
            pltpu.SemaphoreType.DMA((5,)),
            pltpu.SemaphoreType.DMA((MESSAGES,)),
            pltpu.SemaphoreType.DMA((MESSAGES,)),
            pltpu.SemaphoreType.DMA((8,)),
        ],
        compiler_params=pltpu.CompilerParams(collective_id=1, has_side_effects=True, vmem_limit_bytes=60 << 20),
    )(values, hidden, gain, router_t, routes_t, live, wo, win, wout, sin, sout)


def body(
    hidden,
    attn_gain,
    w_query,
    w_latent,
    latent_gain,
    w_key_up,
    w_value_up,
    w_out,
    kv_cache,
    lengths,
    live_mask,
    mlp_gain,
    w_router,
    routes,
    w_experts_in,
    w_experts_out,
    w_shared_in,
    w_shared_out,
):
    request_count = hidden.shape[0]
    local_heads = w_key_up.shape[0]
    cache_length = kv_cache.shape[1]
    gathered, query_all = front(hidden, attn_gain.reshape(1, -1), w_latent.T, w_query)
    query_all = query_all.reshape(request_count, local_heads, NOPE + ROPE)
    positions = lengths.astype(jnp.float32)
    query_nope = query_all[..., :NOPE].astype(jnp.bfloat16)
    query_rope = rotary(query_all[..., NOPE:], positions).astype(jnp.bfloat16)
    query_latent = jnp.einsum(
        "rhn,hnc->rhc", query_nope, w_key_up, preferred_element_type=jnp.float32
    ).astype(jnp.bfloat16)
    width = w_latent.shape[1]
    fresh_kv = jnp.concatenate([gathered[i, :, :width] for i in range(4)], axis=1)
    latent_new = rms_norm(fresh_kv[:, :LAT].astype(jnp.float32), latent_gain)
    rope_new = rotary(fresh_kv[:, LAT:].astype(jnp.float32), positions)
    key_new = jnp.concatenate([latent_new, rope_new], axis=-1).astype(jnp.bfloat16)
    query_full = jnp.concatenate([query_latent, query_rope], axis=-1)
    inverse_root = 1.0 / math.sqrt(NOPE + ROPE)
    scores = (
        jnp.einsum("rhc,rjc->rhj", query_full, kv_cache, preferred_element_type=jnp.float32)
        * inverse_root
    )
    in_cache = jnp.arange(cache_length, dtype=jnp.int32)[None, :] < lengths[:, None]
    scores = jnp.where(in_cache[:, None, :], scores, -jnp.inf)
    score_new = (
        jnp.einsum("rhc,rc->rh", query_full, key_new, preferred_element_type=jnp.float32)
        * inverse_root
    )
    highest = jnp.maximum(jnp.max(scores, axis=-1), score_new)
    weights_cached = jnp.exp(scores - highest[..., None])
    weight_new = jnp.exp(score_new - highest)
    denominator = jnp.sum(weights_cached, axis=-1) + weight_new
    probabilities = (weights_cached / denominator[..., None]).astype(jnp.bfloat16)
    prob_new = (weight_new / denominator).astype(jnp.bfloat16)
    context = jnp.einsum(
        "rhj,rjc->rhc", probabilities, kv_cache[..., :LAT], preferred_element_type=jnp.float32
    )
    context = (
        context
        + prob_new.astype(jnp.float32)[..., None] * key_new[:, None, :LAT].astype(jnp.float32)
    ).astype(jnp.bfloat16)
    values = jnp.einsum(
        "rhc,hcv->rhv", context, w_value_up, preferred_element_type=jnp.float32
    ).astype(jnp.bfloat16)
    experts_in = jnp.transpose(w_experts_in, (0, 2, 3, 1)).reshape(4, 352, 2048)
    shared_in = jnp.transpose(w_shared_in, (1, 2, 0))
    return moe(
        values.reshape(request_count, local_heads * VDIM),
        hidden,
        mlp_gain.reshape(1, -1),
        w_router.T,
        routes.T,
        live_mask.reshape(1, -1),
        w_out,
        experts_in,
        w_experts_out,
        shared_in,
        w_shared_out,
    )


def solution(mesh):
    placed = (
        P("dp", None),
        P(),
        P(None, "head"),
        P(None, "head"),
        P(),
        P("head", None, None),
        P("head", None, None),
        P("head", None),
        P("dp", None, None),
        P("dp"),
        P("dp"),
        P(),
        P(),
        P("dp", None),
        P("dp", None, None, "head"),
        P("dp", "head", None),
        P(None, None, "head"),
        P("head", None),
    )
    return jax.shard_map(
        body, mesh=mesh, in_specs=placed, out_specs=P("dp", "head"), check_vma=False
    )
```

```python
import functools
import math

import jax
import jax.numpy as jnp
from jax import lax
from jax.experimental import pallas as pl
from jax.experimental.pallas import tpu as pltpu
from jax.sharding import PartitionSpec as P

NOPE = 128
ROPE = 64
VDIM = 128
LAT = 512

norm_eps = 1e-06
rope_theta = 50000.0
route_scale = 2.446

MESH = pl.DeviceIdType.MESH
BF = jnp.bfloat16
F32 = jnp.float32
NT = (((1,), (1,)), ((), ()))
TN = (((0,), (0,)), ((), ()))


def rms_norm(values, weights):
    mean_square = jnp.mean(values * values, axis=-1, keepdims=True)
    return values * lax.rsqrt(mean_square + norm_eps) * weights


def rotary(values, positions):
    half_size = values.shape[-1] // 2
    frequency = rope_theta ** (-jnp.arange(half_size, dtype=jnp.float32) / half_size)
    angles = positions.reshape((-1,) + (1,) * (values.ndim - 1)) * frequency
    first_half = values[..., :half_size]
    second_half = values[..., half_size:]
    cosine = jnp.cos(angles)
    sine_part = jnp.sin(angles)
    return jnp.concatenate(
        [
            first_half * cosine - second_half * sine_part,
            second_half * cosine + first_half * sine_part,
        ],
        axis=-1,
    )


def front_kernel(gain_ref, hid_hbm, wlat_hbm, wq_hbm, o_ref, q_ref, hid, wlat, wq, fresh, wsem, ssem, rsem):
    dp, h = lax.axis_index("dp"), lax.axis_index("head")
    loads = [
        pltpu.make_async_copy(s, d, wsem.at[i]) for i, (s, d) in enumerate(((hid_hbm, hid), (wlat_hbm, wlat), (wq_hbm, wq)))
    ]
    for copy in loads:
        copy.start()
    barrier = pltpu.get_barrier_semaphore()
    for k in range(1, 4):
        pl.semaphore_signal(barrier, inc=1, device_id=(dp, lax.rem(h + k, 4)), device_id_type=MESH)
    fresh[...] = jnp.zeros_like(fresh)
    loads[0].wait()
    normed = rms_norm(hid[...].astype(F32), gain_ref[...]).astype(BF)
    width = wlat.shape[0]
    loads[1].wait()
    fresh[:, 0:width] = lax.dot_general(normed, wlat[...], NT, preferred_element_type=F32).astype(BF)
    pl.semaphore_wait(barrier, 3)
    for k in range(1, 4):
        pltpu.make_async_remote_copy(
            src_ref=fresh,
            dst_ref=o_ref.at[h],
            send_sem=ssem.at[k - 1],
            recv_sem=rsem.at[k - 1],
            device_id=(dp, lax.rem(h + k, 4)),
            device_id_type=MESH,
        ).start()
    o_ref[h] = fresh[...]
    loads[2].wait()
    q_ref[...] = jnp.dot(normed, wq[...], preferred_element_type=F32)
    for k in range(1, 4):
        pltpu.make_async_remote_copy(
            src_ref=fresh,
            dst_ref=o_ref.at[lax.rem(h + 4 - k, 4)],
            send_sem=ssem.at[k - 1],
            recv_sem=rsem.at[k - 1],
            device_id=(dp, lax.rem(h + k, 4)),
            device_id_type=MESH,
        ).wait()


def front(hidden, gain, w_latent_t, w_query):
    vmem = pl.BlockSpec(memory_space=pltpu.VMEM)
    rows = hidden.shape[0]
    return pl.pallas_call(
        front_kernel,
        out_shape=(
            jax.ShapeDtypeStruct((4, rows, 256), BF),
            jax.ShapeDtypeStruct((rows, w_query.shape[1]), F32),
        ),
        in_specs=[vmem] + [pl.BlockSpec(memory_space=pltpu.HBM)] * 3,
        out_specs=(vmem, vmem),
        scratch_shapes=[
            pltpu.VMEM(hidden.shape, BF),
            pltpu.VMEM(w_latent_t.shape, BF),
            pltpu.VMEM(w_query.shape, BF),
            pltpu.VMEM((rows, 256), BF),
            pltpu.SemaphoreType.DMA((3,)),
            pltpu.SemaphoreType.DMA((3,)),
            pltpu.SemaphoreType.DMA((3,)),
        ],
        compiler_params=pltpu.CompilerParams(collective_id=0, has_side_effects=True, vmem_limit_bytes=67043328),
    )(gain, hidden, w_latent_t, w_query)


def moe_kernel(
    val_ref, hid_ref, gain_ref, rt_ref, routes_ref, live_ref, wo_hbm, win_hbm, wout_hbm, sin_hbm, sout_hbm,
    out_ref,
    wo, part, win, wout, sin, sout, yrs, mix, ffn, xb, shared, gate_s, xs, hid_slot, outs, pmat, wslot, cb, pr, rl, rf,
    al, af, fr, yr,
    wsem, ssem, rsem, fsem,
):
    dp, h = lax.axis_index("dp"), lax.axis_index("head")
    core = lax.rem(dp, 2)
    x = lax.rem(dp // 2, 4)
    z = dp // 8
    a = x + core * (z - x)
    b = z + core * (x - z)
    sa, sb = 2 + 6 * core, 8 - 6 * core
    na, nb = 1 + 3 * core, 4 - 3 * core

    def dev(da, db):
        return (lax.rem(a + da + 4, 4) * sa + lax.rem(b + db + 4, 4) * sb + core, h)

    def num(da, db):
        return lax.rem(a + da + 4, 4) * na + lax.rem(b + db + 4, 4) * nb

    partner = (dp + 1 - 2 * core, h)

    def ypeer(k):
        return (dp, lax.rem(h + k, 4))

    weights = [
        pltpu.make_async_copy(s, d, wsem.at[i])
        for i, (s, d) in enumerate(
            (
                (sin_hbm, sin),
                (sout_hbm, sout),
                (win_hbm, win),
                (wout_hbm, wout),
            )
        )
    ]
    out_weight = pltpu.make_async_copy(wo_hbm, wo, wsem.at[4])
    for copy in [out_weight] + weights:
        copy.start()

    barrier = pltpu.get_barrier_semaphore()
    other_dp = dp + 1 - 2 * core
    diagonal = tuple((other_dp, lax.rem(h + k, 4)) for k in range(1, 4))
    for peer in (ypeer(1), ypeer(2), ypeer(3), dev(1, 0), dev(-1, 0), dev(0, 1), dev(0, -1), partner) + diagonal:
        pl.semaphore_signal(barrier, inc=1, device_id=peer, device_id_type=MESH)
    out_weight.wait()
    for i in range(4):
        part[i] = jnp.dot(val_ref[...], wo[:, i * 512 : (i + 1) * 512], preferred_element_type=F32).astype(BF)
    pl.semaphore_wait(barrier, 11)

    pending = []

    def send(i, src, dst, peer):
        copy = pltpu.make_async_remote_copy(
            src_ref=src, dst_ref=dst, send_sem=ssem.at[i], recv_sem=rsem.at[i], device_id=peer, device_id_type=MESH
        )
        copy.start()
        pending.append(copy)

    def recv(i, dst):
        pltpu.make_async_remote_copy(
            src_ref=dst, dst_ref=dst, send_sem=ssem.at[i], recv_sem=rsem.at[i], device_id=partner, device_id_type=MESH
        ).wait_recv()

    for k in range(1, 4):
        send(k - 1, part.at[lax.rem(h + k, 4)], yrs.at[k - 1], ypeer(k))
    own = pl.ds(pl.multiple_of(h * 512, 512), 512)
    attention = part[h].astype(F32)
    for k in range(1, 4):
        recv(k - 1, yrs.at[k - 1])
        attention = attention + yrs[k - 1].astype(F32)
    mix[h] = (hid_ref[:, own].astype(F32) + attention).astype(BF)
    for k in range(1, 4):
        send(2 + k, mix.at[h], mix.at[h], ypeer(k))
    for k in range(1, 4):
        recv(2 + k, mix.at[lax.rem(h + 4 - k, 4)])
    square = jnp.zeros((32, 1), F32)
    for i in range(4):
        v = mix[i].astype(F32)
        square = square + jnp.sum(v * v, axis=1, keepdims=True)
    scale = lax.rsqrt(square * (1.0 / 2048.0) + norm_eps)
    for i in range(4):
        v = mix[i].astype(F32)
        ffn[:, i * 512 : (i + 1) * 512] = (v * scale * gain_ref[:, i * 512 : (i + 1) * 512]).astype(BF)

    logits = lax.dot_general(rt_ref[...], ffn[...], NT, preferred_element_type=F32)
    expert_id = lax.broadcasted_iota(jnp.int32, (64, 32), 0)
    named = expert_id == routes_ref[0:1, :]
    for k in range(1, 6):
        named = named | (expert_id == routes_ref[k : k + 1, :])
    chosen = jnp.where(named, jax.nn.sigmoid(logits), 0.0)
    weight = route_scale * live_ref[...].astype(F32) * chosen / jnp.sum(chosen, axis=0, keepdims=True)
    w_hi = weight.astype(BF)
    w_lo = (weight - w_hi.astype(F32)).astype(BF)
    eye = (lax.broadcasted_iota(jnp.int32, (32, 32), 0) == lax.broadcasted_iota(jnp.int32, (32, 32), 1)).astype(F32).astype(BF)
    extra = lax.dot_general(eye, jnp.concatenate([w_hi, w_lo], axis=0), NT, preferred_element_type=F32).astype(BF)

    me = num(0, 0)
    rows = pl.ds(pl.multiple_of(me * 64 + core * 32, 32), 32)
    for half in range(2):
        xb[half, rows, 0:1024] = ffn[:, half * 1024 : (half + 1) * 1024]
        xb[half, rows, 1024:1152] = extra

    def block(n, low=0, count=64):
        return xb.at[core, pl.ds(pl.multiple_of(n * 64 + low, 32), count), :]

    def other(n):
        return xb.at[1 - core, pl.ds(pl.multiple_of(n * 64, 32), 64), :]

    G = 8
    PT = G + 20
    send(PT, xb.at[1 - core, rows, :], xb.at[1 - core, rows, :], partner)
    send(PT + 1, xb.at[core, rows, :], xb.at[core, rows, :], partner)
    prow = pl.ds(pl.multiple_of(me * 64 + (1 - core) * 32, 32), 32)
    recv(PT, xb.at[core, prow, :])

    order = (0, -1, 1, 2)

    def spread(j):
        base = G + 4 + 4 * j
        send(base, block(num(order[j], 0)), block(num(order[j], 0)), dev(0, 1))
        send(base + 1, block(num(order[j], 0)), block(num(order[j], 0)), dev(0, -1))

    def to_partner(j, o):
        if (j, o) != (0, 0):
            n = num(order[j], order[o])
            send(PT + 1 + 4 * j + o, block(n), block(n), partner)

    send(G, block(me), block(me), dev(1, 0))
    send(G + 1, block(me), block(me), dev(-1, 0))
    spread(0)

    weights[0].wait()
    weights[1].wait()

    def shared_gate():
        gate_s[...] = lax.dot_general(ffn[...], sin[0], NT, preferred_element_type=F32)

    def shared_up():
        gate = gate_s[...]
        up = lax.dot_general(ffn[...], sin[1], NT, preferred_element_type=F32)
        hid_slot[0:32, :] = (gate / (1.0 + jnp.exp(-gate)) * up).astype(BF)

    def shared_down(i):
        shared[i] = jnp.dot(
            hid_slot[0:32, :], sout[:, i * 512 : (i + 1) * 512], preferred_element_type=F32
        ).astype(BF)

    shared_gate()
    recv(G, block(num(-1, 0)))
    n = num(-1, 0)
    send(G + 2, block(n, 0, 32), block(n, 0, 32), dev(1, 0))
    spread(1)
    recv(G + 1, block(num(1, 0)))
    n = num(1, 0)
    send(G + 3, block(n, 32, 32), block(n, 32, 32), dev(-1, 0))
    spread(2)
    shared_up()

    def first(j):
        base = G + 4 + 4 * j
        n = num(order[j], -1)
        recv(base, block(n))
        send(base + 2, block(n, 0, 32), block(n, 0, 32), dev(0, 1))
        n = num(order[j], 1)
        recv(base + 1, block(n))
        send(base + 3, block(n, 32, 32), block(n, 32, 32), dev(0, -1))
        to_partner(j, 1)
        to_partner(j, 2)

    def second(j):
        base = G + 4 + 4 * j
        n = num(order[j], 2)
        recv(base + 2, block(n, 0, 32))
        recv(base + 3, block(n, 32, 32))
        to_partner(j, 3)

    first(0)
    recv(G + 2, block(num(2, 0), 0, 32))
    recv(G + 3, block(num(2, 0), 32, 32))
    spread(3)
    for j in range(1, 4):
        to_partner(j, 0)
    shared_down(0)
    first(1)
    shared_down(1)
    first(2)
    shared_down(2)
    second(0)
    shared_down(3)
    first(3)
    F = PT + 17 + 4 + 20
    for k in range(1, 4):
        send(F + k, shared.at[lax.rem(h + k, 4)], yr.at[k - 1], ypeer(k))
    second(1)
    second(2)
    second(3)

    prow2 = pl.ds(pl.multiple_of(me * 64 + (1 - core) * 32, 32), 32)
    recv(PT + 1, xb.at[1 - core, prow2, :])
    for j in range(4):
        for o in range(4):
            if (j, o) != (0, 0):
                recv(PT + 1 + 4 * j + o, other(num(order[o], order[j])))

    lane = lax.broadcasted_iota(jnp.int32, (8, 128), 1)
    row = lax.broadcasted_iota(jnp.int32, (8, 128), 0)
    target = 2 * dp + lax.rem(row, 2) + 64 * (row // 2)
    pick = jnp.where((lane == target) & (row < 4), 1.0, 0.0).astype(BF)
    t_from = lax.broadcasted_iota(jnp.int32, (256, 256), 0)
    t_to = lax.broadcasted_iota(jnp.int32, (256, 256), 1)
    before = jnp.where((t_from < t_to) & (t_from // 32 == t_to // 32), 1.0, 0.0).astype(BF)
    source = lax.broadcasted_iota(jnp.int32, (1, 256), 1) // 32
    slot = lax.broadcasted_iota(jnp.int32, (64, 256), 0)
    for g in range(4):
        info = lax.dot_general(pick, xb[0, g * 256 : (g + 1) * 256, 1024:1152], NT, preferred_element_type=F32)
        mask = jnp.where(info != 0.0, 1.0, 0.0)
        rank = jnp.dot(mask.astype(BF), before, preferred_element_type=F32)
        for e in range(2):
            value = info[e : e + 1, :] + info[2 + e : 3 + e, :]
            place = jnp.where(mask[e : e + 1, :] > 0.0, 8 * source + rank[e : e + 1, :].astype(jnp.int32), -1)
            hit = jnp.where(slot == place, 1.0, 0.0)
            wslot[e, g * 64 : (g + 1) * 64, :] = jnp.broadcast_to(
                jnp.sum(hit * value, axis=1, keepdims=True), (64, 128)
            )
            hit = hit.astype(BF)
            pmat[g, e * 64 : (e + 1) * 64, :] = hit
        for half in range(2):
            got = jnp.dot(
                pmat[g], xb[half, g * 256 : (g + 1) * 256, 0:1024], preferred_element_type=F32
            ).astype(BF)
            for e in range(2):
                xs[e, g * 64 : (g + 1) * 64, half * 1024 : (half + 1) * 1024] = got[e * 64 : (e + 1) * 64]

    weights[2].wait()
    weights[3].wait()
    for e in range(2):
        gate = lax.dot_general(xs[e], win[2 * e], NT, preferred_element_type=F32)
        up = lax.dot_general(xs[e], win[2 * e + 1], NT, preferred_element_type=F32)
        hid_slot[...] = (gate / (1.0 + jnp.exp(-gate)) * up).astype(BF)
        for i in range(4):
            result = jnp.dot(hid_slot[...], wout[e, :, i * 512 : (i + 1) * 512], preferred_element_type=F32)
            result = (result * wslot[e, :, 0:1]).astype(BF)
            for g in range(4):
                outs[g, e * 64 : (e + 1) * 64, i * 512 : (i + 1) * 512] = result[g * 64 : (g + 1) * 64]

    R = PT + 17
    for g in range(4):
        for half in range(2):
            cb[half, g * 256 : (g + 1) * 256, :] = lax.dot_general(
                pmat[g], outs[g, :, half * 1024 : (half + 1) * 1024], TN, preferred_element_type=F32
            ).astype(BF)
        span = pl.ds(g * 256, 256)
        send(R + g, cb.at[1 - core, span, :], pr.at[span, :], partner)
    for g in range(4):
        span = pl.ds(g * 256, 256)
        recv(R + g, pr.at[span, :])
        cb[core, span, :] = (cb[core, span, :].astype(F32) + pr[span, :].astype(F32)).astype(BF)

    def cpart(n, low=0, count=64):
        return pl.ds(pl.multiple_of(n * 64 + low, 32), count)

    def ring(base, here, ahead, behind, far, up_dev, down_dev, lows, fulls, stage):
        if stage == 0:
            send(base, cb.at[core, cpart(far, 0, 32), :], lows.at[0], up_dev)
            send(base + 1, cb.at[core, cpart(far, 32, 32), :], lows.at[1], down_dev)
        elif stage == 1:
            recv(base, lows.at[0])
            s = cpart(ahead, 0, 32)
            cb[core, s, :] = (cb[core, s, :].astype(F32) + lows[0].astype(F32)).astype(BF)
            send(base + 2, cb.at[core, cpart(ahead), :], fulls.at[0], up_dev)
            recv(base + 1, lows.at[1])
            s = cpart(behind, 32, 32)
            cb[core, s, :] = (cb[core, s, :].astype(F32) + lows[1].astype(F32)).astype(BF)
            send(base + 3, cb.at[core, cpart(behind), :], fulls.at[1], down_dev)
        else:
            recv(base + 2, fulls.at[0])
            recv(base + 3, fulls.at[1])
            s = cpart(here)
            cb[core, s, :] = (cb[core, s, :].astype(F32) + fulls[0].astype(F32) + fulls[1].astype(F32)).astype(BF)

    S = R + 4
    back = (2, 1, -1, 0)

    def bring(j, stage):
        d = back[j]
        ring(S + 4 * j, num(d, 0), num(d, 1), num(d, -1), num(d, 2), dev(0, 1), dev(0, -1), rl.at[j], rf.at[j], stage)

    def aring(stage):
        ring(S + 16, num(0, 0), num(1, 0), num(-1, 0), num(2, 0), dev(1, 0), dev(-1, 0), al, af, stage)

    for j in range(4):
        bring(j, 0)
    for j in range(4):
        bring(j, 1)
    bring(0, 2)
    aring(0)
    bring(1, 2)
    bring(2, 2)
    aring(1)
    bring(3, 2)
    aring(2)

    local = []
    for q in range(2):
        owner = 2 * core + q
        for t, (span, where) in enumerate(((rows, dp), (prow, other_dp))):
            copy = pltpu.make_async_remote_copy(
                src_ref=cb.at[core, span, pl.ds(q * 512, 512)],
                dst_ref=fr.at[h],
                send_sem=fsem.at[2 * q + t],
                recv_sem=fsem.at[4 + h],
                device_id=(where, owner),
                device_id_type=MESH,
            )
            if t == 1:
                copy.start()
                pending.append(copy)
            else:
                pl.when(owner != h)(copy.start)
                local.append((owner, copy))
    result = mix[h].astype(F32) + shared[h].astype(F32)
    for k in range(1, 4):
        recv(F + k, yr.at[k - 1])
        result = result + yr[k - 1].astype(F32)

    def routed_recv(o):
        pltpu.make_async_remote_copy(
            src_ref=fr.at[o],
            dst_ref=fr.at[o],
            send_sem=fsem.at[0],
            recv_sem=fsem.at[4 + o],
            device_id=partner,
            device_id_type=MESH,
        ).wait_recv()

    mine = core == h // 2

    @pl.when(mine)
    def _():
        fr[h] = cb[core, rows, pl.ds(pl.multiple_of(lax.rem(h, 2) * 512, 512), 512)]

    @pl.when(jnp.logical_not(mine))
    def _():
        routed_recv(h)

    for k in range(1, 4):
        routed_recv(lax.rem(h + k, 4))
    for i in range(4):
        result = result + fr[i].astype(F32)
    out_ref[...] = result.astype(BF)
    for copy in pending:
        copy.wait_send()
    for owner, copy in local:
        pl.when(owner != h)(copy.wait_send)


MESSAGES = 8 + 20 + 17 + 4 + 20 + 4


def moe(values, hidden, gain, router_t, routes_t, live, wo, win, wout, sin, sout):
    vmem = pl.BlockSpec(memory_space=pltpu.VMEM)
    hbm = pl.BlockSpec(memory_space=pl.ANY)
    return pl.pallas_call(
        moe_kernel,
        out_shape=jax.ShapeDtypeStruct((32, 512), BF),
        in_specs=[vmem] * 6 + [hbm] * 5,
        out_specs=vmem,
        scratch_shapes=[
            pltpu.VMEM((512, 2048), BF),
            pltpu.VMEM((4, 32, 512), BF),
            pltpu.VMEM((4, 352, 2048), BF),
            pltpu.VMEM((2, 352, 2048), BF),
            pltpu.VMEM((2, 352, 2048), BF),
            pltpu.VMEM((352, 2048), BF),
            pltpu.VMEM((3, 32, 512), BF),
            pltpu.VMEM((4, 32, 512), BF),
            pltpu.VMEM((32, 2048), BF),
            pltpu.VMEM((2, 1024, 1152), BF),
            pltpu.VMEM((4, 32, 512), BF),
            pltpu.VMEM((32, 352), F32),
            pltpu.VMEM((2, 256, 2048), BF),
            pltpu.VMEM((256, 352), BF),
            pltpu.VMEM((4, 128, 2048), BF),
            pltpu.VMEM((4, 128, 256), BF),
            pltpu.VMEM((2, 256, 128), F32),
            pltpu.VMEM((2, 1024, 1024), BF),
            pltpu.VMEM((1024, 1024), BF),
            pltpu.VMEM((4, 2, 32, 1024), BF),
            pltpu.VMEM((4, 2, 64, 1024), BF),
            pltpu.VMEM((2, 32, 1024), BF),
            pltpu.VMEM((2, 64, 1024), BF),
            pltpu.VMEM((4, 32, 512), BF),
            pltpu.VMEM((3, 32, 512), BF),
            pltpu.SemaphoreType.DMA((5,)),
            pltpu.SemaphoreType.DMA((MESSAGES,)),
            pltpu.SemaphoreType.DMA((MESSAGES,)),
            pltpu.SemaphoreType.DMA((8,)),
        ],
        compiler_params=pltpu.CompilerParams(collective_id=1, has_side_effects=True, vmem_limit_bytes=60 << 20),
    )(values, hidden, gain, router_t, routes_t, live, wo, win, wout, sin, sout)


def body(
    hidden,
    attn_gain,
    w_query,
    w_latent,
    latent_gain,
    w_key_up,
    w_value_up,
    w_out,
    kv_cache,
    lengths,
    live_mask,
    mlp_gain,
    w_router,
    routes,
    w_experts_in,
    w_experts_out,
    w_shared_in,
    w_shared_out,
):
    request_count = hidden.shape[0]
    local_heads = w_key_up.shape[0]
    cache_length = kv_cache.shape[1]
    gathered, query_all = front(hidden, attn_gain.reshape(1, -1), w_latent.T, w_query)
    query_all = query_all.reshape(request_count, local_heads, NOPE + ROPE)
    positions = lengths.astype(jnp.float32)
    query_nope = query_all[..., :NOPE].astype(jnp.bfloat16)
    query_rope = rotary(query_all[..., NOPE:], positions).astype(jnp.bfloat16)
    query_latent = jnp.einsum(
        "rhn,hnc->rhc", query_nope, w_key_up, preferred_element_type=jnp.float32
    ).astype(jnp.bfloat16)
    width = w_latent.shape[1]
    fresh_kv = jnp.concatenate([gathered[i, :, :width] for i in range(4)], axis=1)
    latent_new = rms_norm(fresh_kv[:, :LAT].astype(jnp.float32), latent_gain)
    rope_new = rotary(fresh_kv[:, LAT:].astype(jnp.float32), positions)
    key_new = jnp.concatenate([latent_new, rope_new], axis=-1).astype(jnp.bfloat16)
    query_full = jnp.concatenate([query_latent, query_rope], axis=-1)
    inverse_root = 1.0 / math.sqrt(NOPE + ROPE)
    scores = (
        jnp.einsum("rhc,rjc->rhj", query_full, kv_cache, preferred_element_type=jnp.float32)
        * inverse_root
    )
    in_cache = jnp.arange(cache_length, dtype=jnp.int32)[None, :] < lengths[:, None]
    scores = jnp.where(in_cache[:, None, :], scores, -jnp.inf)
    score_new = (
        jnp.einsum("rhc,rc->rh", query_full, key_new, preferred_element_type=jnp.float32)
        * inverse_root
    )
    highest = jnp.maximum(jnp.max(scores, axis=-1), score_new)
    weights_cached = jnp.exp(scores - highest[..., None])
    weight_new = jnp.exp(score_new - highest)
    denominator = jnp.sum(weights_cached, axis=-1) + weight_new
    probabilities = (weights_cached / denominator[..., None]).astype(jnp.bfloat16)
    prob_new = (weight_new / denominator).astype(jnp.bfloat16)
    context = jnp.einsum(
        "rhj,rjc->rhc", probabilities, kv_cache[..., :LAT], preferred_element_type=jnp.float32
    )
    context = (
        context
        + prob_new.astype(jnp.float32)[..., None] * key_new[:, None, :LAT].astype(jnp.float32)
    ).astype(jnp.bfloat16)
    values = jnp.einsum(
        "rhc,hcv->rhv", context, w_value_up, preferred_element_type=jnp.float32
    ).astype(jnp.bfloat16)
    experts_in = jnp.transpose(w_experts_in, (0, 2, 3, 1)).reshape(4, 352, 2048)
    shared_in = jnp.transpose(w_shared_in, (1, 2, 0))
    return moe(
        values.reshape(request_count, local_heads * VDIM),
        hidden,
        mlp_gain.reshape(1, -1),
        w_router.T,
        routes.T,
        live_mask.reshape(1, -1),
        w_out,
        experts_in,
        w_experts_out,
        shared_in,
        w_shared_out,
    )


def solution(mesh):
    placed = (
        P("dp", None),
        P(),
        P(None, "head"),
        P(None, "head"),
        P(),
        P("head", None, None),
        P("head", None, None),
        P("head", None),
        P("dp", None, None),
        P("dp"),
        P("dp"),
        P(),
        P(),
        P("dp", None),
        P("dp", None, None, "head"),
        P("dp", "head", None),
        P(None, None, "head"),
        P("head", None),
    )
    return jax.shard_map(
        body, mesh=mesh, in_specs=placed, out_specs=P("dp", "head"), check_vma=False
    )
```
